32 devices in a mesh: fsdp: 4 (over x, core), tensor: 2 (over y), dp: 4 (over z).
Axes of the slice: x: 2, y: 2, z: 4, core: 2. Of those that a mesh axis runs over, the one named last changes fastest.
Arguments:
- grad_part: bfloat16 [32, 2, 2, 16, 8192], P(('fsdp', 'tensor', 'dp')), may hold values from -6 to 6
- policy: float32 [2, 2, 16, 8192], P(None, None, None, ('fsdp', 'tensor')), may hold values from -6 to 6
- ref_old: float32 [2, 2, 16, 8192], P(None, None, None, ('fsdp', 'tensor')), may hold values from -6 to 6
- hidden_base: bfloat16 [4, 2, 64, 8192], P('dp', None, None, 'fsdp'), may hold values from -40 to 40
- norm_gain: float32 [8192], replicated, may hold values from 0.5 to 1.5
- unembed: bfloat16 [8192, 3072], P(None, ('fsdp', 'tensor')), may hold values from -1 to 1
- token_ids: int32 [4, 2, 64], P('dp'), may hold values from 0 to 3071
- prompt_mask: int32 [4, 2, 64], P('dp'), may hold values from 0 to 1, as said below
- resp_len: int32 [4, 2], P('dp'), may hold values from 16 to 48
Outputs:
- ref_next: float32 [2, 2, 16, 8192], P(None, None, None, ('fsdp', 'tensor'))
- token_logp: float32 [4, 2, 64], P('dp')
- seq_mean: float32 [4, 2], P('dp')
The draws below stay inside these ranges and needn't reach their ends.
Inputs may be any that keep to these rules, and one draw needn't show every extreme that they name: `prompt_mask`: each sequence's mask is 1 on a prefix of 8 to 16 positions and 0 after it.
All inputs are finite; a program needn't handle non-finite values.
Results may differ from the reference program's by a relative error of at most 0.0013.
Values may be sent and summed in bfloat16 or wider, within the bound.
A program may use at most 64 MiB of HBM per device.

```python
import math
import jax
import jax.numpy as jnp
import numpy as np
from jax import lax

D = 8192
V_DEV = 384
R = 16
LAYERS = 2
SEQ = 64
VOCAB = 3072
PARTIALS = 32
N_FSDP = 4
N_TENSOR = 2
N_DP = 4


def draw_unembed(key, part):
    column_scale = 4.0 / math.sqrt(D)
    drawn = jnp.clip(jax.random.normal(jax.random.fold_in(key, 1), (D, VOCAB), jnp.float32), -6.0, 6.0) * column_scale
    return drawn.astype(jnp.bfloat16)


def draw_hidden_base(key, part):
    drawn = jnp.clip(jax.random.normal(jax.random.fold_in(key, 4), (N_DP, 2, SEQ, D), jnp.float32), -6.0, 6.0)
    return drawn.astype(jnp.bfloat16)


def draw_prompt_mask(key, part):
    lengths = jax.random.randint(jax.random.fold_in(key, 21), (N_DP, 2), SEQ // 8, SEQ // 4 + 1)
    position = jnp.arange(SEQ, dtype=jnp.int32)
    return (position[None, None, :] < lengths[:, :, None]).astype(jnp.int32)


def plant(values, stream_key, least, high):
    place = [jax.random.randint(jax.random.fold_in(stream_key, axis), (), 0, length) for axis, length in enumerate(values.shape)]
    widest = values.shape.index(max(values.shape))
    next_to = place[:widest] + [(place[widest] + 1) % values.shape[widest]] + place[widest + 1:]
    return values.at[tuple(place)].set(least).at[tuple(next_to)].set(high)


def strengthened(result, key, source, target, shards_of, factor):
    def block_of(dim):
        return (jnp.arange(result.shape[dim]) // (result.shape[dim] // shards_of)).reshape((-1,) + (1,) * (result.ndim - 1 - dim))

    near = jax.random.permutation(key, shards_of)[block_of(target)]
    far = (block_of(target) + shards_of // 2) % shards_of
    return jnp.where((block_of(source) == near) | (block_of(source) == far), factor * result, result)


def level_of(stream_key, dims, split, least, top_value):
    level = 1.0
    for axis_at, shards_of in split:
        heights = jax.random.uniform(jax.random.fold_in(jax.random.fold_in(stream_key, 6), axis_at), (shards_of,), jnp.float32, least / len(split), top_value / len(split))
        level = level * jnp.repeat(jnp.exp(heights), dims[axis_at] // shards_of).reshape((-1,) + (1,) * (len(dims) - 1 - axis_at))
    return level


def rank_table(count, slope):
    portions = [(1 << 20) // math.isqrt(rank ** slope) + 1 for rank in range(1, count + 1)]
    scale = 1 + sum(portions) // (1 << 30)
    return np.cumsum(np.array([max(1, weight // scale) for weight in portions]))


def ranked_ids(rng, extent, number_of, skew):
    grid = rank_table(number_of, skew)
    pick = jax.random.randint(jax.random.fold_in(rng, 1), extent, 0, int(grid[number_of - 1]))
    grade = jnp.searchsorted(jnp.asarray(grid, jnp.int32), pick, side="right")
    return jax.random.permutation(jax.random.fold_in(rng, 2), number_of)[grade].astype(jnp.int32)


def scatter_about(own_key, shape, scale, limit, split=(), kind=jnp.bfloat16):
    values = jax.random.normal(own_key, shape, jnp.float32) * scale
    if len(split) > 0:
        values = level_of(own_key, shape, split, -0.22, 0.18) * values
    return jnp.clip(values, min=-limit, max=limit).astype(kind)


def gaussian_with(stream_key, dims, spread, reach, shards, heavy, kind=jnp.bfloat16):
    values = spread * jax.random.normal(stream_key, dims, jnp.float32)
    if shards:
        values = values * level_of(stream_key, dims, shards, -0.22, 0.18)
    return jnp.clip(strengthened(values, jax.random.fold_in(stream_key, 3), *heavy), -reach, reach).astype(kind)


def setup_inputs(seed: int = 0) -> dict:
    splits = jax.random.split(jax.random.key(seed), 10)
    grad_part = gaussian_with(splits[0], (PARTIALS, LAYERS, 2, R, D), 1.0, 6.0, ((0, 32),), (0, 4, 32, 2.75))
    policy = scatter_about(splits[1], (LAYERS, 2, R, D), 1.0, 6.0, ((3, 8),), jnp.float32)
    ref_old = scatter_about(splits[2], (LAYERS, 2, R, D), 1.0, 6.0, ((3, 8),), jnp.float32)
    hidden_base = draw_hidden_base(jax.random.fold_in(splits[9], 71), 0)
    norm_gain = jnp.clip(1.0 + 0.1 * jax.random.normal(splits[4], (D,), jnp.float32), 0.5, 1.5)
    unembed = draw_unembed(jax.random.fold_in(splits[9], 71), 0)
    token_ids = plant(ranked_ids(splits[6], (N_DP, 2, SEQ), VOCAB, 2), jax.random.fold_in(splits[6], 3), 0, VOCAB - 1).astype(jnp.int32)
    prompt_mask = draw_prompt_mask(jax.random.fold_in(splits[9], 71), 0)
    resp_len = plant(jax.random.randint(splits[8], (N_DP, 2), SEQ // 4, 3 * SEQ // 4 + 1), jax.random.fold_in(splits[8], 1), SEQ // 4, (3 * SEQ // 4 + 1) - 1).astype(jnp.int32)
    return {"grad_part": grad_part, "policy": policy, "ref_old": ref_old, "hidden_base": hidden_base, "norm_gain": norm_gain, "unembed": unembed, "token_ids": token_ids, "prompt_mask": prompt_mask, "resp_len": resp_len}


def reference(grad_part, policy, ref_old, hidden_base, norm_gain, unembed, token_ids, prompt_mask, resp_len):
    grad_mean = lax.optimization_barrier(jnp.sum(grad_part, axis=0, dtype=jnp.float32)) / PARTIALS
    ref_next = 0.4 * ref_old + 0.6 * (policy - 8.0 * grad_mean)
    adapter = ref_old[LAYERS - 1].astype(jnp.bfloat16)
    row_total = N_DP * 2 * SEQ
    flat_rows = hidden_base.reshape(row_total, D)
    low_rank = (lax.dot_general(flat_rows, adapter[0], (((1,), (1,)), ((), ())), preferred_element_type=jnp.float32) / math.sqrt(D)).astype(jnp.bfloat16)
    hidden = flat_rows.astype(jnp.float32) + jnp.dot(low_rank, adapter[1], preferred_element_type=jnp.float32) / math.sqrt(R)
    normed = (hidden * lax.rsqrt(lax.optimization_barrier(jnp.mean(hidden * hidden, axis=1, keepdims=True)) + 1e-05) * norm_gain).astype(jnp.bfloat16)
    flat_ids = token_ids.reshape(row_total).astype(jnp.int32)
    block_width = V_DEV * N_TENSOR
    column_iota = jnp.arange(block_width, dtype=jnp.int32)

    def step_block(block_index, running):
        top_prev, exp_prev, target_prev = running
        offset = (block_index * block_width).astype(jnp.int32)
        weights = lax.dynamic_slice_in_dim(unembed, offset, block_width, 1)
        logits = jnp.dot(normed, weights, preferred_element_type=jnp.float32)
        new_top = jnp.maximum(top_prev, lax.optimization_barrier(jnp.max(logits, axis=1)))
        exp_next = exp_prev * jnp.exp(top_prev - new_top) + lax.optimization_barrier(jnp.sum(jnp.exp(logits - new_top[:, None]), axis=1))
        local_ids = flat_ids - offset
        is_target = column_iota[None, :] == local_ids[:, None]
        target_next = target_prev + lax.optimization_barrier(jnp.sum(jnp.where(is_target, logits, 0.0), axis=1))
        return (new_top, exp_next, target_next)
    empty_rows = jnp.zeros((row_total,), jnp.float32)
    start_state = (jnp.full((row_total,), -jnp.inf, jnp.float32), empty_rows, empty_rows)
    top_all, exp_all, target_all = lax.fori_loop(0, N_FSDP, step_block, start_state)
    log_total = top_all + jnp.log(exp_all)
    token_all = (target_all - log_total).reshape(N_DP, 2, SEQ)
    prompt_len = lax.optimization_barrier(jnp.sum(prompt_mask, axis=2, keepdims=True))
    position = jnp.arange(SEQ, dtype=jnp.int32)[None, None, :]
    resp_mask = (prompt_mask == 0) & (position < prompt_len + resp_len[:, :, None])
    token_logp = jnp.where(resp_mask, token_all, 0.0)
    seq_mean = lax.optimization_barrier(jnp.sum(token_logp, axis=2)) / resp_len.astype(jnp.float32)
    return (ref_next, token_logp, seq_mean)
```

```python
import functools
import math

import jax
import jax.numpy as jnp
from jax import lax
from jax.experimental import pallas as pl
from jax.experimental.pallas import tpu as pltpu
from jax.sharding import PartitionSpec as P

D = 8192
R = 16


def merged(value, axis, join):
    pieces = jax.tree.map(lambda part: lax.all_gather(part, axis), value)
    head = jax.tree.map(lambda part: part[0], pieces)
    tail = jax.tree.map(lambda part: part[1:], pieces)
    subtotal, _ = lax.scan(lambda subtotal, share: (join(subtotal, share), None), head, tail)
    return subtotal


def combine_stats(left_stats, right_stats):
    new_top = jnp.maximum(left_stats[0], right_stats[0])
    summed = left_stats[1] * jnp.exp(left_stats[0] - new_top) + right_stats[1] * jnp.exp(
        right_stats[0] - new_top
    )
    return (new_top, summed, left_stats[2] + right_stats[2])


def per_device(
    grad_part, policy, ref_old, hidden_base, norm_gain, unembed, token_ids, prompt_mask, resp_len
):
    grad_terms = grad_part[0].astype(jnp.float32)
    device_total = lax.axis_size("fsdp") * lax.axis_size("tensor") * lax.axis_size("dp")
    grad_scale = 8.0 / device_total
    grad_piece = lax.psum_scatter(grad_terms, ("fsdp", "tensor"), scatter_dimension=3, tiled=True)
    grad_total = lax.psum(grad_piece, "dp")
    ref_next = 0.4 * ref_old + 0.6 * (policy - grad_scale * grad_total)
    adapter = ref_old[ref_old.shape[0] - 1].astype(jnp.bfloat16)
    adapter_full = lax.all_gather(adapter, ("fsdp", "tensor"), axis=2, tiled=True)
    base_full = lax.all_gather(hidden_base, "fsdp", axis=3, tiled=True)
    feature_count = base_full.shape[3]
    flat_rows = base_full.reshape(-1, feature_count)
    low_rank = (
        lax.dot_general(
            flat_rows, adapter_full[0], (((1,), (1,)), ((), ())), preferred_element_type=jnp.float32
        )
        / math.sqrt(D)
    ).astype(jnp.bfloat16)
    hidden = flat_rows.astype(jnp.float32) + jnp.dot(
        low_rank, adapter_full[1], preferred_element_type=jnp.float32
    ) / math.sqrt(R)
    normed = (
        hidden * lax.rsqrt(jnp.mean(hidden * hidden, axis=1, keepdims=True) + 1e-05) * norm_gain
    ).astype(jnp.bfloat16)
    vocab_width = unembed.shape[1]
    column_start = (
        lax.axis_index("fsdp") * lax.axis_size("tensor") + lax.axis_index("tensor")
    ) * vocab_width
    column_iota = jnp.arange(vocab_width, dtype=jnp.int32)
    logits = jnp.dot(normed, unembed, preferred_element_type=jnp.float32)
    top_row = jnp.max(logits, axis=1)
    exp_row = jnp.sum(jnp.exp(logits - top_row[:, None]), axis=1)
    local_ids = token_ids.reshape(-1) - column_start
    is_target = column_iota[None, :] == local_ids[:, None]
    target_row = jnp.sum(jnp.where(is_target, logits, 0.0), axis=1)
    top_all, exp_all, target_all = merged(
        (top_row, exp_row, target_row), ("fsdp", "tensor"), combine_stats
    )
    log_total = top_all + jnp.log(exp_all)
    token_all = (target_all - log_total).reshape(token_ids.shape)
    seq_length = token_all.shape[2]
    prompt_len = jnp.sum(prompt_mask, axis=2, keepdims=True)
    position = jnp.arange(seq_length, dtype=jnp.int32)[None, None, :]
    resp_mask = (prompt_mask == 0) & (position < prompt_len + resp_len[:, :, None])
    token_logp = jnp.where(resp_mask, token_all, 0.0)
    seq_mean = jnp.sum(token_logp, axis=2) / resp_len.astype(jnp.float32)
    return (ref_next, token_logp, seq_mean)


MESH = pl.DeviceIdType.MESH
LIMIT = 32767.0


def coded(value):
    top = jnp.maximum(jnp.max(jnp.abs(value), axis=0, keepdims=True), 1e-30)
    return jnp.round(value * (LIMIT / top)).astype(jnp.int16), top * (1.0 / LIMIT)


def decoded(code, step):
    return code.astype(jnp.float32) * step


WINDOW = 48
ROWS = 2 * WINDOW


def window_rows(mask):
    start = jnp.sum(mask.astype(jnp.float32), axis=1, keepdims=True)
    row = lax.broadcasted_iota(jnp.int32, (ROWS, 128), 0)
    place = lax.broadcasted_iota(jnp.int32, (ROWS, 128), 1).astype(jnp.float32)
    source = row.astype(jnp.float32) + jnp.where(row < WINDOW, start[0:1], start[1:2] + (64.0 - WINDOW))
    return jnp.where(place == source, 1.0, 0.0)


def fused_kernel(
    grad_scale,
    grad_hbm, policy_hbm, ref_hbm, base_hbm, gain_hbm, unembed_hbm, ids_hbm, mask_hbm, len_hbm,
    next_ref, token_ref, mean_ref,
    unembed, base, gain, policy, ref_old, ids, mask, lens,
    grad_all, grad_in, pick, packed, row_ids, first_code, first_step, first_in_code, first_in_step,
    second_code, second_step, second_in_code, second_in_step, plane,
    part_code, part_step, share_code, share_step, total_code, total_step,
    low_rank, low_turned, fold, up_map, squares, normed, stats,
    load_sem, core_send, core_recv, first_send, first_recv, second_send, second_recv,
    share_send, share_recv,
    total_send, total_recv, low_send, low_recv, map_sem, square_send, square_recv,
    feed_send, feed_recv, stat_send, stat_recv,
):
    f, t, z = lax.axis_index("fsdp"), lax.axis_index("tensor"), lax.axis_index("dp")
    x, c = f // 2, f % 2
    me = f * 2 + t
    z_high, z_low = z // 2, z % 2

    def flip(bit, by):
        return bit + by - 2 * bit * by

    def plane_peer(r):
        return {
            "fsdp": flip(x, r // 4) * 2 + flip(c, (r // 2) % 2),
            "tensor": flip(t, r % 2),
            "dp": z,
        }

    def stack_peer(r):
        return flip(z_high, r // 2) * 2 + flip(z_low, r % 2)

    def at_stack(index):
        return {"fsdp": f, "tensor": t, "dp": index}

    sibling, x_peer, y_peer = plane_peer(2), plane_peer(4), plane_peer(1)
    f_core, f_x, f_far = sibling["fsdp"], x_peer["fsdp"], plane_peer(6)["fsdp"]

    def remote(src, dst, send, recv, peer):
        return pltpu.make_async_remote_copy(
            src_ref=src, dst_ref=dst, send_sem=send, recv_sem=recv, device_id=peer,
            device_id_type=MESH,
        )

    def lanes(start, size):
        return pl.ds(pl.multiple_of(start, 128), size)

    loads = [
        pltpu.make_async_copy(src, dst, load_sem.at[i])
        for i, (src, dst) in enumerate(
            [
                (mask_hbm, mask),
                (ids_hbm, ids),
                (base_hbm, base),
                (ref_hbm, ref_old),
                (grad_hbm.at[:, lanes(flip(x, 1) * 4096, 4096)], grad_all.at[1]),
                (grad_hbm.at[:, lanes(x * 4096, 4096)], grad_all.at[0]),
                (gain_hbm.at[:, lanes(f * 2048, 2048)], gain),
                (len_hbm, lens),
                (unembed_hbm, unembed),
                (policy_hbm, policy),
            ]
        )
    ]
    for load in loads[:8]:
        load.start()

    barrier = pltpu.get_barrier_semaphore()
    for r in range(1, 8):
        pl.semaphore_signal(barrier, inc=1, device_id=plane_peer(r), device_id_type=MESH)
    for r in range(1, 4):
        pl.semaphore_signal(
            barrier, inc=1, device_id=at_stack(stack_peer(r)), device_id_type=MESH
        )

    loads[0].wait()
    loads[1].wait()
    chosen = window_rows(mask[...])
    pick[...] = chosen.astype(jnp.bfloat16)
    id_row = jnp.concatenate([ids[0:1, :], ids[1:2, :]], axis=1).astype(jnp.float32)
    id_rows = lax.dot_general(
        jnp.broadcast_to(id_row, (8, 128)), chosen, (((1,), (1,)), ((), ())),
        preferred_element_type=jnp.float32, precision=lax.Precision.HIGHEST,
    )
    row_ids[...] = id_rows[0:1].astype(jnp.int32)
    piece = 512
    loads[2].wait()
    for i in range(2048 // piece):
        cols = slice(i * piece, (i + 1) * piece)
        packed[:, cols] = jnp.dot(
            pick[...], base[:, cols], preferred_element_type=jnp.float32
        ).astype(jnp.bfloat16)
    for load in loads[8:]:
        load.start()
    loads[3].wait()
    up_map[t] = ref_old[48:64, :].astype(jnp.bfloat16)
    down = ref_old[32:48, :].astype(jnp.bfloat16)
    low_rank[me] = lax.dot_general(
        down, packed[:, lanes(t * 1024, 1024)], (((1,), (1,)), ((), ())),
        preferred_element_type=jnp.float32,
    )
    loads[4].wait()
    loads[5].wait()
    pl.semaphore_wait(barrier, 10)

    sent = []

    def go(copy):
        copy.start()
        sent.append(copy)
        return copy

    wide, width = 512, 256
    pairs = [(1, 1), (1, 0), (0, 1), (0, 0)]

    def place(core, dt, k):
        return core * 2048 + flip(t, dt) * 1024 + k * wide

    core_copies = [{}, {}]

    def core_exchange(k):
        for dx, dt in pairs:
            slot = dx * 2 + dt
            core_copies[k][slot] = go(
                remote(
                    grad_all.at[dx, :, lanes(place(1 - c, dt, k), wide)], grad_in.at[k, slot],
                    core_send.at[k, slot], core_recv.at[k, slot], sibling,
                )
            )

    core_exchange(0)

    low_copies = [
        go(
            remote(
                low_rank.at[me], low_rank.at[me], low_send.at[r], low_recv.at[r], plane_peer(r)
            )
        )
        for r in (5, 7, 4, 6, 1, 3, 2)
    ]

    map_copy = go(remote(up_map.at[t], up_map.at[t], map_sem.at[0], map_sem.at[1], y_peer))
    core_exchange(1)

    def chip_sum(dx, dt, k, side):
        own = grad_all[dx, :, lanes(place(c, dt, k) + side * width, width)]
        other = grad_in[k, dx * 2 + dt, :, side * width : (side + 1) * width]
        return own.astype(jnp.float32) + other.astype(jnp.float32)

    def both(out_code, out_step, in_code, in_step, send, recv, side, k, peer):
        return [
            go(remote(out.at[side, k], into.at[side, k], send.at[side, k, i], recv.at[side, k, i], peer))
            for i, (out, into) in enumerate([(out_code, in_code), (out_step, in_step)])
        ]

    first_copies, second_copies = {}, {}

    def first(k):
        for slot in (3, 2, 1):
            core_copies[k][slot].wait_recv()
        for side, peer in ((0, x_peer), (1, y_peer)):
            for j in range(2):
                dx, dt = (1, j) if side == 0 else (j, 1)
                code, step = coded(chip_sum(dx, dt, k, side))
                first_code[side, k, :, j * width : (j + 1) * width] = code
                first_step[side, k, :, j * width : (j + 1) * width] = step
            first_copies[side, k] = both(
                first_code, first_step, first_in_code, first_in_step, first_send, first_recv, side, k, peer
            )

    def first_total(side, k, j):
        dx, dt = (0, j) if side == 0 else (j, 0)
        cols = slice(j * width, (j + 1) * width)
        return chip_sum(dx, dt, k, side) + decoded(
            first_in_code[side, k, :, cols], first_in_step[side, k, :, cols]
        )

    def second(k):
        core_copies[k][0].wait_recv()
        for side, peer in ((0, y_peer), (1, x_peer)):
            for copy in first_copies[side, k]:
                copy.wait_recv()
            code, step = coded(first_total(side, k, 1))
            second_code[side, k] = code
            second_step[side, k] = step
            second_copies[side, k] = both(
                second_code, second_step, second_in_code, second_in_step, second_send, second_recv,
                side, k, peer,
            )

    first(0)
    first(1)

    for copy in low_copies:
        copy.wait_recv()
    map_copy.wait_recv()
    rank_sum = low_rank[0]
    for p in range(1, 8):
        rank_sum = rank_sum + low_rank[p]
    rank_sum = (rank_sum * (1.0 / math.sqrt(D))).astype(jnp.bfloat16).astype(jnp.float32)
    loads[6].wait()

    low_turned[...] = rank_sum.T.astype(jnp.bfloat16)

    def correct(half):
        part = pl.ds(pl.multiple_of(half * WINDOW, 16), WINDOW)
        total = jnp.zeros((WINDOW, 128), jnp.float32)
        for i in range(2048 // piece):
            cols = slice(i * piece, (i + 1) * piece)
            inner = (i * piece) % 1024
            step = jnp.dot(
                low_turned[part, :], up_map[(i * piece) // 1024, :, inner : inner + piece],
                preferred_element_type=jnp.float32,
            )
            hidden = packed[part, cols].astype(jnp.float32) + step * (1.0 / math.sqrt(R))
            normed[f, part, cols] = (hidden * gain[:, cols]).astype(jnp.bfloat16)
            square = hidden * hidden
            for j in range(piece // 128):
                total = total + square[:, j * 128 : (j + 1) * 128]
        fold[part, :] = total

    chunks = WINDOW // 16

    def feed(src_f, half, k, slot, peer):
        block = normed.at[src_f, pl.ds(pl.multiple_of(half * WINDOW + k * 16, 16), 16)]
        return go(remote(block, block, feed_send.at[slot], feed_recv.at[slot], peer))

    correct(t)
    from_x = [feed(f, t, k, k, x_peer) for k in range(chunks)]
    correct(1 - t)
    own_block = normed.at[f]
    from_core = go(remote(own_block, own_block, feed_send.at[3], feed_recv.at[3], sibling))
    squares[f] = jnp.sum(fold[...].T, axis=0, keepdims=True)
    square_copies = [
        go(
            remote(
                squares.at[f], squares.at[f], square_send.at[i], square_recv.at[i], plane_peer(r)
            )
        )
        for i, r in enumerate((2, 4, 6))
    ]

    second(0)
    second(1)

    share_copies = [[], []]

    def half_lanes(h):
        return slice(h * wide, (h + 1) * wide)

    def share(h):
        for side in range(2):
            for copy in second_copies[side, h]:
                copy.wait_recv()
            cols = slice(h * wide + side * width, h * wide + (side + 1) * width)
            value = first_total(side, h, 0) + decoded(
                second_in_code[side, h], second_in_step[side, h]
            )
            plane[:, cols] = value
            for q in range(4):
                code, step = coded(value[q * 16 : (q + 1) * 16])
                part_code[q, :, cols] = code
                part_step[q, :, cols] = step
        part = half_lanes(h)
        for r in (3, 2, 1):
            other = stack_peer(r)
            for i, (out, into) in enumerate([(part_code, share_code), (part_step, share_step)]):
                share_copies[h].append(
                    go(remote(out.at[other, :, part], into.at[r - 1, :, part], share_send.at[h, i, r - 1], share_recv.at[h, i, r - 1], at_stack(other)))
                )

    total_copies = []

    def finish(h):
        for copy in share_copies[h]:
            copy.wait_recv()
        part = half_lanes(h)
        value = plane[pl.ds(pl.multiple_of(z * 16, 16), 16), part]
        for slot in range(3):
            value = value + decoded(share_code[slot, :, part], share_step[slot, :, part])
        code, step = coded(value)
        total_code[z, :, part] = code
        total_step[z, :, part] = step
        for r in (3, 2, 1):
            peer = at_stack(stack_peer(r))
            for i, kind in enumerate([total_code, total_step]):
                block = kind.at[z, :, part]
                total_copies.append(
                    go(remote(block, block, total_send.at[h, i, r - 1], total_recv.at[h, i, r - 1], peer))
                )

    def product(index):
        return jnp.dot(
            normed[index], unembed[pl.ds(pl.multiple_of(index * 2048, 2048), 2048), :],
            preferred_element_type=jnp.float32,
        )

    from_y, from_side = [], []

    def pass_on(k):
        from_x[k].wait_recv()
        from_y.append(feed(f_x, t, k, 4 + k, y_peer))
        from_side.append(feed(f_x, t, k, 7 + k, sibling))

    loads[8].wait()
    logits = product(f)
    pass_on(0)
    share(0)
    pass_on(1)
    share(1)
    pass_on(2)
    from_core.wait_recv()
    logits = logits + product(f_core)
    finish(0)
    for k in range(chunks):
        from_y[k].wait_recv()
        from_side.append(feed(f_x, 1 - t, k, 10 + k, sibling))
    logits = logits + product(f_x)
    finish(1)
    for copy in from_side:
        copy.wait_recv()
    logits = logits + product(f_far)

    for copy in square_copies:
        copy.wait_recv()
    square_sum = squares[0]
    for p in range(1, 4):
        square_sum = square_sum + squares[p]
    logits = logits.T * lax.rsqrt(square_sum * (1.0 / D) + 1e-05)
    top = jnp.max(logits, axis=0, keepdims=True)
    local_ids = row_ids[...] - me * logits.shape[0]
    index = lax.broadcasted_iota(jnp.int32, logits.shape, 0)
    stats[me, 0:1, :] = top
    stats[me, 1:2, :] = jnp.sum(jnp.exp(logits - top), axis=0, keepdims=True)
    stats[me, 2:3, :] = jnp.sum(jnp.where(index == local_ids, logits, 0.0), axis=0, keepdims=True)
    stats[me, 3:8, :] = jnp.zeros((5, ROWS), jnp.float32)
    stat_copies = [
        go(remote(stats.at[me], stats.at[me], stat_send.at[r], stat_recv.at[r], plane_peer(r)))
        for r in (5, 7, 4, 6, 1, 3, 2)
    ]

    loads[7].wait()
    loads[9].wait()
    for copy in total_copies:
        copy.wait_recv()
    for q in range(4):
        part = slice(q * 16, (q + 1) * 16)
        total = decoded(total_code[q], total_step[q])
        next_ref[part, :] = 0.4 * ref_old[part, :] + 0.6 * (policy[part, :] - grad_scale * total)

    for copy in sent[: -len(stat_copies)]:
        copy.wait_send()
    for copy in stat_copies:
        copy.wait_recv()
    every = [stats[p] for p in range(8)]
    top = functools.reduce(jnp.maximum, [one[0:1] for one in every])
    exp_sum = functools.reduce(jnp.add, [one[1:2] * jnp.exp(one[0:1] - top) for one in every])
    target = functools.reduce(jnp.add, [one[2:3] for one in every])
    token = target - (top + jnp.log(exp_sum))
    high = token.astype(jnp.bfloat16).astype(jnp.float32)
    middle = (token - high).astype(jnp.bfloat16).astype(jnp.float32)
    thirds = jnp.concatenate([high, middle, token - high - middle, jnp.zeros((5, ROWS), jnp.float32)], axis=0)
    spread = jnp.sum(
        jnp.dot(thirds.astype(jnp.bfloat16), pick[...], preferred_element_type=jnp.float32),
        axis=0, keepdims=True,
    )
    token = jnp.concatenate([spread[:, :64], spread[:, 64:]], axis=0)
    prompt = mask[...]
    prompt_len = jnp.sum(prompt.astype(jnp.float32), axis=1, keepdims=True)
    resp = jnp.concatenate([lens[0:1, 0:1], lens[0:1, 1:2]], axis=0).astype(jnp.float32)
    position = lax.broadcasted_iota(jnp.int32, prompt.shape, 1).astype(jnp.float32)
    token = jnp.where((prompt == 0) & (position < prompt_len + resp), token, 0.0)
    token_ref[...] = token
    mean = jnp.sum(token, axis=1, keepdims=True) / resp
    mean_ref[...] = jnp.concatenate([mean[0:1], mean[1:2]], axis=1)

    for copy in stat_copies:
        copy.wait_send()


def kept_kernel(*refs):
    half = len(refs) // 2
    for source, result in zip(refs[:half], refs[half:]):
        result[...] = source[...]


def kept(arrays):
    block = pl.BlockSpec(memory_space=pltpu.VMEM)
    return pl.pallas_call(
        kept_kernel,
        out_shape=[jax.ShapeDtypeStruct(one.shape, one.dtype) for one in arrays],
        in_specs=[block] * len(arrays),
        out_specs=[block] * len(arrays),
        compiler_params=pltpu.CompilerParams(vmem_limit_bytes=8 * 1024 * 1024),
    )(*arrays)


def fused(
    grad_part, policy, ref_old, hidden_base, norm_gain, unembed, token_ids, prompt_mask, resp_len
):
    f32, bf16, i16, i32 = jnp.float32, jnp.bfloat16, jnp.int16, jnp.int32
    device_total = lax.axis_size("fsdp") * lax.axis_size("tensor") * lax.axis_size("dp")
    dma = pltpu.SemaphoreType.DMA
    outs = pl.pallas_call(
        functools.partial(fused_kernel, 8.0 / device_total),
        out_shape=[
            pltpu.VMEM((64, 1024), f32),
            pltpu.VMEM((2, 64), f32),
            pltpu.VMEM((1, 2), f32),
        ],
        in_specs=[pl.BlockSpec(memory_space=pl.ANY)] * 9,
        out_specs=[pl.BlockSpec(memory_space=pltpu.VMEM)] * 3,
        scratch_shapes=[
            pltpu.VMEM(unembed.shape, bf16),
            pltpu.VMEM((128, 2048), bf16),
            pltpu.VMEM((1, 2048), f32),
            pltpu.VMEM((64, 1024), f32),
            pltpu.VMEM((64, 1024), f32),
            pltpu.VMEM((2, 64), i32),
            pltpu.VMEM((2, 64), i32),
            pltpu.VMEM((1, 2), i32),
            pltpu.VMEM((2, 64, 4096), bf16),
            pltpu.VMEM((2, 4, 64, 512), bf16),
            pltpu.VMEM((ROWS, 128), bf16),
            pltpu.VMEM((ROWS, 2048), bf16),
            pltpu.VMEM((1, ROWS), i32),
            pltpu.VMEM((2, 2, 64, 512), i16),
            pltpu.VMEM((2, 2, 1, 512), f32),
            pltpu.VMEM((2, 2, 64, 512), i16),
            pltpu.VMEM((2, 2, 1, 512), f32),
            pltpu.VMEM((2, 2, 64, 256), i16),
            pltpu.VMEM((2, 2, 1, 256), f32),
            pltpu.VMEM((2, 2, 64, 256), i16),
            pltpu.VMEM((2, 2, 1, 256), f32),
            pltpu.VMEM((64, 1024), f32),
            pltpu.VMEM((4, 16, 1024), i16),
            pltpu.VMEM((4, 1, 1024), f32),
            pltpu.VMEM((3, 16, 1024), i16),
            pltpu.VMEM((3, 1, 1024), f32),
            pltpu.VMEM((4, 16, 1024), i16),
            pltpu.VMEM((4, 1, 1024), f32),
            pltpu.VMEM((8, 16, ROWS), f32),
            pltpu.VMEM((ROWS, 16), bf16),
            pltpu.VMEM((ROWS, 128), f32),
            pltpu.VMEM((2, 16, 1024), bf16),
            pltpu.VMEM((4, 1, ROWS), f32),
            pltpu.VMEM((4, ROWS, 2048), bf16),
            pltpu.VMEM((8, 8, ROWS), f32),
            dma((10,)), dma((2, 4)), dma((2, 4)), dma((2, 2, 2)), dma((2, 2, 2)), dma((2, 2, 2)), dma((2, 2, 2)),
            dma((2, 2, 3)), dma((2, 2, 3)),
            dma((2, 2, 3)), dma((2, 2, 3)), dma((8,)), dma((8,)), dma((2,)), dma((3,)), dma((3,)),
            dma((13,)), dma((13,)), dma((8,)), dma((8,)),
        ],
        compiler_params=pltpu.CompilerParams(
            collective_id=0, has_side_effects=True, vmem_limit_bytes=56 * 1024 * 1024
        ),
    )(
        grad_part.reshape(64, 8192),
        policy.reshape(64, 1024),
        ref_old.reshape(64, 1024),
        hidden_base.reshape(128, 2048),
        norm_gain.reshape(1, 8192),
        unembed,
        token_ids.reshape(2, 64),
        prompt_mask.reshape(2, 64),
        resp_len,
    )
    outs = kept(outs)
    return (outs[0].reshape(policy.shape), outs[1].reshape(token_ids.shape), outs[2])


def solution(mesh):
    planes = (mesh.shape["fsdp"], mesh.shape["tensor"], mesh.shape["dp"])
    return jax.shard_map(
        fused if planes == (4, 2, 4) else per_device,
        mesh=mesh,
        in_specs=(
            P(("fsdp", "tensor", "dp"), None, None, None, None),
            P(None, None, None, ("fsdp", "tensor")),
            P(None, None, None, ("fsdp", "tensor")),
            P("dp", None, None, "fsdp"),
            P(),
            P(None, ("fsdp", "tensor")),
            P("dp", None, None),
            P("dp", None, None),
            P("dp", None),
        ),
        out_specs=(P(None, None, None, ("fsdp", "tensor")), P("dp", None, None), P("dp", None)),
        check_vma=False,
    )
```

```python
import functools
import math

import jax
import jax.numpy as jnp
from jax import lax
from jax.experimental import pallas as pl
from jax.experimental.pallas import tpu as pltpu
from jax.sharding import PartitionSpec as P

D = 8192
R = 16


def merged(value, axis, join):
    pieces = jax.tree.map(lambda part: lax.all_gather(part, axis), value)
    head = jax.tree.map(lambda part: part[0], pieces)
    tail = jax.tree.map(lambda part: part[1:], pieces)
    subtotal, _ = lax.scan(lambda subtotal, share: (join(subtotal, share), None), head, tail)
    return subtotal


def combine_stats(left_stats, right_stats):
    new_top = jnp.maximum(left_stats[0], right_stats[0])
    summed = left_stats[1] * jnp.exp(left_stats[0] - new_top) + right_stats[1] * jnp.exp(
        right_stats[0] - new_top
    )
    return (new_top, summed, left_stats[2] + right_stats[2])


def per_device(
    grad_part, policy, ref_old, hidden_base, norm_gain, unembed, token_ids, prompt_mask, resp_len
):
    grad_terms = grad_part[0].astype(jnp.float32)
    device_total = lax.axis_size("fsdp") * lax.axis_size("tensor") * lax.axis_size("dp")
    grad_scale = 8.0 / device_total
    grad_piece = lax.psum_scatter(grad_terms, ("fsdp", "tensor"), scatter_dimension=3, tiled=True)
    grad_total = lax.psum(grad_piece, "dp")
    ref_next = 0.4 * ref_old + 0.6 * (policy - grad_scale * grad_total)
    adapter = ref_old[ref_old.shape[0] - 1].astype(jnp.bfloat16)
    adapter_full = lax.all_gather(adapter, ("fsdp", "tensor"), axis=2, tiled=True)
    base_full = lax.all_gather(hidden_base, "fsdp", axis=3, tiled=True)
    feature_count = base_full.shape[3]
    flat_rows = base_full.reshape(-1, feature_count)
    low_rank = (
        lax.dot_general(
            flat_rows, adapter_full[0], (((1,), (1,)), ((), ())), preferred_element_type=jnp.float32
        )
        / math.sqrt(D)
    ).astype(jnp.bfloat16)
    hidden = flat_rows.astype(jnp.float32) + jnp.dot(
        low_rank, adapter_full[1], preferred_element_type=jnp.float32
    ) / math.sqrt(R)
    normed = (
        hidden * lax.rsqrt(jnp.mean(hidden * hidden, axis=1, keepdims=True) + 1e-05) * norm_gain
    ).astype(jnp.bfloat16)
    vocab_width = unembed.shape[1]
    column_start = (
        lax.axis_index("fsdp") * lax.axis_size("tensor") + lax.axis_index("tensor")
    ) * vocab_width
    column_iota = jnp.arange(vocab_width, dtype=jnp.int32)
    logits = jnp.dot(normed, unembed, preferred_element_type=jnp.float32)
    top_row = jnp.max(logits, axis=1)
    exp_row = jnp.sum(jnp.exp(logits - top_row[:, None]), axis=1)
    local_ids = token_ids.reshape(-1) - column_start
    is_target = column_iota[None, :] == local_ids[:, None]
    target_row = jnp.sum(jnp.where(is_target, logits, 0.0), axis=1)
    top_all, exp_all, target_all = merged(
        (top_row, exp_row, target_row), ("fsdp", "tensor"), combine_stats
    )
    log_total = top_all + jnp.log(exp_all)
    token_all = (target_all - log_total).reshape(token_ids.shape)
    seq_length = token_all.shape[2]
    prompt_len = jnp.sum(prompt_mask, axis=2, keepdims=True)
    position = jnp.arange(seq_length, dtype=jnp.int32)[None, None, :]
    resp_mask = (prompt_mask == 0) & (position < prompt_len + resp_len[:, :, None])
    token_logp = jnp.where(resp_mask, token_all, 0.0)
    seq_mean = jnp.sum(token_logp, axis=2) / resp_len.astype(jnp.float32)
    return (ref_next, token_logp, seq_mean)


MESH = pl.DeviceIdType.MESH
LIMIT = 32767.0


def coded(value):
    top = jnp.maximum(jnp.max(jnp.abs(value), axis=0, keepdims=True), 1e-30)
    return jnp.round(value * (LIMIT / top)).astype(jnp.int16), top * (1.0 / LIMIT)


def decoded(code, step):
    return code.astype(jnp.float32) * step


WINDOW = 48
ROWS = 2 * WINDOW


def window_rows(mask):
    start = jnp.sum(mask.astype(jnp.float32), axis=1, keepdims=True)
    row = lax.broadcasted_iota(jnp.int32, (ROWS, 128), 0)
    place = lax.broadcasted_iota(jnp.int32, (ROWS, 128), 1).astype(jnp.float32)
    source = row.astype(jnp.float32) + jnp.where(row < WINDOW, start[0:1], start[1:2] + (64.0 - WINDOW))
    return jnp.where(place == source, 1.0, 0.0)


PARTS = 4
WIDE = 1024 // PARTS
WIDTH = WIDE // 2
FEEDS = 4
SPAN = 2048 // FEEDS


def fused_kernel(
    grad_scale,
    grad_hbm, policy_hbm, ref_hbm, base_hbm, gain_hbm, unembed_hbm, ids_hbm, mask_hbm, len_hbm,
    next_ref, token_ref, mean_ref,
    unembed, base, gain, policy, ref_old, ids, mask, lens,
    grad_all, grad_in, pick, packed, row_ids, first_code, first_step, first_in_code, first_in_step,
    second_code, second_step, second_in_code, second_in_step, plane,
    part_code, part_step, share_code, share_step, total_code, total_step,
    low_rank, squares, normed, stats,
    load_sem, core_send, core_recv, first_send, first_recv, second_send, second_recv,
    share_send, share_recv, total_send, total_recv, low_send, low_recv, square_send, square_recv,
    side_send, side_recv, map_send, map_recv, x_send, x_recv, y_send, y_recv,
    own_send, own_recv, far_send, far_recv, stat_send, stat_recv,
):
    f, t, z = lax.axis_index("fsdp"), lax.axis_index("tensor"), lax.axis_index("dp")
    x, c = f // 2, f % 2
    me = f * 2 + t
    z_high, z_low = z // 2, z % 2

    def flip(bit, by):
        return bit + by - 2 * bit * by

    inner = flip(z_high, z_low)
    half = z_high
    slot_of = z_high + z_high + inner - 2 * z_high * inner

    def plane_peer(r):
        return {
            "fsdp": flip(x, r // 4) * 2 + flip(c, (r // 2) % 2),
            "tensor": flip(t, r % 2),
            "dp": z,
        }

    def stack_peer(r):
        return flip(z_high, r // 2) * 2 + flip(z_low, r % 2)

    def at_stack(index):
        return {"fsdp": f, "tensor": t, "dp": index}

    sibling, x_peer, y_peer = plane_peer(2), plane_peer(4), plane_peer(1)
    f_core, f_x, f_far = sibling["fsdp"], x_peer["fsdp"], plane_peer(6)["fsdp"]
    far_first = (5, 7, 4, 6, 1, 3, 2)

    def remote(src, dst, send, recv, peer):
        return pltpu.make_async_remote_copy(
            src_ref=src, dst_ref=dst, send_sem=send, recv_sem=recv, device_id=peer,
            device_id_type=MESH,
        )

    def lanes(start, size):
        return pl.ds(pl.multiple_of(start, 128), size)

    loads = [
        pltpu.make_async_copy(src, dst, load_sem.at[i])
        for i, (src, dst) in enumerate(
            [
                (mask_hbm, mask),
                (ids_hbm, ids),
                (base_hbm, base),
                (gain_hbm.at[:, lanes(f * 2048, 2048)], gain),
                (ref_hbm, ref_old),
                (grad_hbm.at[:, lanes(flip(x, 1) * 4096, 4096)], grad_all.at[1]),
                (grad_hbm.at[:, lanes(x * 4096, 4096)], grad_all.at[0]),
                (len_hbm, lens),
                (unembed_hbm, unembed),
                (policy_hbm, policy),
            ]
        )
    ]
    for load in loads[:8]:
        load.start()

    barrier = pltpu.get_barrier_semaphore()
    for r in range(1, 3):
        pl.semaphore_signal(
            barrier, inc=1, device_id=at_stack(stack_peer(r)), device_id_type=MESH
        )

    @pl.when(inner == 1)
    def _():
        pl.semaphore_signal(
            barrier, inc=1, device_id=at_stack(stack_peer(3)), device_id_type=MESH
        )

    for r in far_first:
        pl.semaphore_signal(barrier, inc=1, device_id=plane_peer(r), device_id_type=MESH)

    loads[0].wait()
    loads[1].wait()
    chosen = window_rows(mask[...])
    pick[...] = chosen.astype(jnp.bfloat16)
    id_row = jnp.concatenate([ids[0:1, :], ids[1:2, :]], axis=1).astype(jnp.float32)
    id_rows = lax.dot_general(
        jnp.broadcast_to(id_row, (8, 128)), chosen, (((1,), (1,)), ((), ())),
        preferred_element_type=jnp.float32, precision=lax.Precision.HIGHEST,
    )
    row_ids[...] = id_rows[0:1].astype(jnp.int32)
    loads[2].wait()
    loads[3].wait()
    for i in range(4):
        cols = slice(i * 512, (i + 1) * 512)
        rows = jnp.dot(pick[...], base[:, cols], preferred_element_type=jnp.float32)
        packed[:, cols] = rows.astype(jnp.bfloat16)
        normed[f, 0:ROWS, cols] = (rows * gain[:, cols]).astype(jnp.bfloat16)
    for load in loads[8:]:
        load.start()
    loads[4].wait()
    mine = lanes(t * 1024, 1024)
    map_rows = pl.ds(ROWS, R)
    up = ref_old[48:64, :].astype(jnp.bfloat16)
    down = ref_old[32:48, :].astype(jnp.bfloat16)
    normed[f, ROWS : ROWS + R, mine] = (up.astype(jnp.float32) * gain[:, mine]).astype(jnp.bfloat16)
    low_rank[0] = lax.dot_general(
        down, packed[:, mine], (((1,), (1,)), ((), ())), preferred_element_type=jnp.float32
    )
    loads[5].wait()
    loads[6].wait()
    pl.semaphore_wait(barrier, 9 + inner)

    sent = []

    def go(copy):
        copy.start()
        sent.append(copy)
        return copy

    pairs = [(1, 1), (1, 0), (0, 1), (0, 0)]

    def place(core, dt, k):
        return core * 2048 + flip(t, dt) * 1024 + k * WIDE

    core_copies = [{} for _ in range(PARTS)]

    def core_exchange(k):
        for dx, dt in pairs:
            slot = dx * 2 + dt
            core_copies[k][slot] = go(
                remote(
                    grad_all.at[dx, :, lanes(place(1 - c, dt, k), WIDE)], grad_in.at[k, slot],
                    core_send.at[k, slot], core_recv.at[k, slot], sibling,
                )
            )

    def rows_of(part):
        return pl.ds(pl.multiple_of(part * WINDOW, 16), WINDOW)

    def feed(src_f, part, q, send, recv, peer):
        block = normed.at[src_f, rows_of(part), q * SPAN : (q + 1) * SPAN]
        return go(remote(block, block, send, recv, peer))

    def feed_map(src_f, part, i, peer):
        block = normed.at[src_f, map_rows, lanes(part * 1024, 1024)]
        return go(remote(block, block, map_send.at[i], map_recv.at[i], peer))

    def exchange(buffer, send, recv):
        return [
            go(remote(buffer.at[me], buffer.at[me], send.at[r], recv.at[r], plane_peer(r)))
            for r in far_first
        ]

    for k in range(PARTS):
        core_exchange(k)
    from_x = [feed(f, t, 0, x_send.at[0], x_recv.at[0], x_peer)]

    def low_step(i, peer):
        return go(
            remote(low_rank.at[2 * i], low_rank.at[2 * i + 1], low_send.at[i], low_recv.at[i], peer)
        )

    low_copies = [low_step(0, sibling)]
    own_rows = normed.at[f, 0:ROWS]
    from_core = go(remote(own_rows, own_rows, own_send.at[0], own_recv.at[0], sibling))

    def low_next(i, peer):
        low_copies[i - 1].wait_recv()
        low_rank[2 * i] = low_rank[2 * i - 2] + low_rank[2 * i - 1]
        low_copies.append(low_step(i, peer))

    def chip_sum(dx, dt, k, side):
        own = grad_all[dx, :, lanes(place(c, dt, k) + side * WIDTH, WIDTH)]
        other = grad_in[k, dx * 2 + dt, :, side * WIDTH : (side + 1) * WIDTH]
        return own.astype(jnp.float32) + other.astype(jnp.float32)

    def both(out_code, out_step, in_code, in_step, send, recv, side, k, peer):
        return [
            go(remote(out.at[side, k], into.at[side, k], send.at[side, k, i], recv.at[side, k, i], peer))
            for i, (out, into) in enumerate([(out_code, in_code), (out_step, in_step)])
        ]

    first_copies, second_copies = {}, {}

    def first(k):
        for slot in (3, 2, 1):
            core_copies[k][slot].wait_recv()
        for side, peer in ((0, x_peer), (1, y_peer)):
            for j in range(2):
                dx, dt = (1, j) if side == 0 else (j, 1)
                code, step = coded(chip_sum(dx, dt, k, side))
                first_code[side, k, :, j * WIDTH : (j + 1) * WIDTH] = code
                first_step[side, k, :, j * WIDTH : (j + 1) * WIDTH] = step
            first_copies[side, k] = both(
                first_code, first_step, first_in_code, first_in_step, first_send, first_recv, side, k, peer
            )

    def first_total(side, k, j):
        dx, dt = (0, j) if side == 0 else (j, 0)
        cols = slice(j * WIDTH, (j + 1) * WIDTH)
        return chip_sum(dx, dt, k, side) + decoded(
            first_in_code[side, k, :, cols], first_in_step[side, k, :, cols]
        )

    def second(k):
        core_copies[k][0].wait_recv()
        for side, peer in ((0, y_peer), (1, x_peer)):
            for copy in first_copies[side, k]:
                copy.wait_recv()
            code, step = coded(first_total(side, k, 1))
            second_code[side, k] = code
            second_step[side, k] = step
            second_copies[side, k] = both(
                second_code, second_step, second_in_code, second_in_step, second_send, second_recv,
                side, k, peer,
            )

    kinds = [(part_code, share_code), (part_step, share_step)]

    def share_copy(k, i, m, slot, target):
        out, into = kinds[i]
        return remote(
            out.at[m, k], into.at[slot, k], share_send.at[k, i, m], share_recv.at[k, i, slot], at_stack(target)
        )

    def total_copy(k, i, r, m):
        block = (total_code, total_step)[i].at[m, k]
        return remote(
            block, block, total_send.at[k, i, r - 1], total_recv.at[k, i, m], at_stack(stack_peer(r))
        )

    def share(k):
        for side in range(2):
            for copy in second_copies[side, k]:
                copy.wait_recv()
            cols = slice(side * WIDTH, (side + 1) * WIDTH)
            value = first_total(side, k, 0) + decoded(
                second_in_code[side, k], second_in_step[side, k]
            )
            plane[k, :, cols] = value
            for m in range(2):
                code, step = coded(value[m * 32 : (m + 1) * 32])
                part_code[m, k, :, cols] = code
                part_step[m, k, :, cols] = step

        @pl.when(inner == 0)
        def _():
            for m in range(2):
                for i in range(2):
                    share_copy(k, i, m, slot_of, 1 + m).start()

        @pl.when(inner == 1)
        def _():
            for i in range(2):
                share_copy(k, i, 1 - half, slot_of, 2 - half).start()

    def finish(k):
        @pl.when(inner == 1)
        def _():
            for slot in (1, 0, 2):
                for i in range(2):
                    share_copy(k, i, 1 - half, slot, 2 - half).wait_recv()
            value = plane[k, pl.ds(pl.multiple_of(half * 32, 32), 32), :]
            for slot in range(3):
                value = value + decoded(share_code[slot, k], share_step[slot, k])
            code, step = coded(value)
            total_code[half, k] = code
            total_step[half, k] = step
            for r in (1, 2, 3):
                for i in range(2):
                    total_copy(k, i, r, half).start()

    def blend(k):
        @pl.when(inner == 0)
        def _():
            for m in range(2):
                for i in range(2):
                    total_copy(k, i, 1, m).wait_recv()

        @pl.when(inner == 1)
        def _():
            for i in range(2):
                total_copy(k, i, 1, 1 - half).wait_recv()

        cols = slice(k * WIDE, (k + 1) * WIDE)
        for m in range(2):
            part = slice(m * 32, (m + 1) * 32)
            total = decoded(total_code[m, k], total_step[m, k])
            next_ref[part, cols] = 0.4 * ref_old[part, cols] + 0.6 * (
                policy[part, cols] - grad_scale * total
            )

    def product(index, q):
        rows = pl.ds(pl.multiple_of(index * 2048 + q * SPAN, SPAN), SPAN)
        return jnp.dot(
            normed[index, :, q * SPAN : (q + 1) * SPAN], unembed[rows, :],
            preferred_element_type=jnp.float32,
        )

    from_y, from_side = [], []

    def pass_on(q):
        from_x[q].wait_recv()
        from_y.append(feed(f_x, t, q, y_send.at[q], y_recv.at[q], y_peer))
        from_side.append(feed(f_x, t, q, side_send.at[q], side_recv.at[q], sibling))

    from_far = []

    def feed_whole(src_f, send, recv, peer):
        block = normed.at[src_f, 0:ROWS, 2048 - SPAN : 2048]
        return go(remote(block, block, send, recv, peer))

    def pass_far(q):
        from_y[q].wait_recv()
        from_far.append(feed(f_x, 1 - t, q, far_send.at[q], far_recv.at[q], sibling))

    def gather(q):
        from_side[q].wait_recv()
        from_far[q].wait_recv()
        return product(f_x, q) + product(f_far, q)
    first(0)
    first(1)
    first(2)
    first(3)
    from_x.append(feed(f, t, 1, x_send.at[1], x_recv.at[1], x_peer))
    pass_on(0)
    low_next(1, x_peer)
    second(0)
    second(1)
    from_x.append(feed(f, t, 2, x_send.at[2], x_recv.at[2], x_peer))
    map_y = feed_map(f, t, 0, y_peer)
    map_core = feed_map(f, t, 2, sibling)
    second(2)
    second(3)
    map_x = feed_map(f, t, 1, x_peer)
    from_x.append(feed_whole(f, x_send.at[3], x_recv.at[3], x_peer))
    pass_on(1)
    share(0)
    share(1)
    low_next(2, y_peer)
    pass_on(2)
    share(2)
    share(3)
    pass_far(0)
    map_y.wait_recv()
    map_side = feed_map(f, 1 - t, 3, sibling)
    map_x.wait_recv()
    map_xy = feed_map(f_x, t, 4, y_peer)
    map_xc = feed_map(f_x, t, 5, sibling)
    loads[8].wait()
    logits = product(f, 0)
    for q in range(1, FEEDS):
        logits = logits + product(f, q)
    for copy in (from_core, map_core, map_side):
        copy.wait_recv()
    for q in range(FEEDS):
        logits = logits + product(f_core, q)
    low_copies[2].wait_recv()
    rank_sum = low_rank[4] + low_rank[5]
    turned = (rank_sum * (1.0 / math.sqrt(D))).T.astype(jnp.bfloat16)
    part_sum = jnp.zeros((ROWS, 128), jnp.float32)
    for i in range(2):
        cols = slice(i * 512, (i + 1) * 512)
        hidden = packed[:, lanes(t * 1024 + i * 512, 512)].astype(jnp.float32) + jnp.dot(
            turned, up[:, cols], preferred_element_type=jnp.float32
        ) * (1.0 / math.sqrt(R))
        square = hidden * hidden
        for j in range(4):
            part_sum = part_sum + square[:, j * 128 : (j + 1) * 128]
    squares[me] = jnp.sum(part_sum.T, axis=0, keepdims=True)
    square_copies = exchange(squares, square_send, square_recv)
    pass_far(1)
    from_x[3].wait_recv()
    whole_side = feed_whole(f_x, side_send.at[3], side_recv.at[3], sibling)
    map_xy.wait_recv()
    map_far = feed_map(f_x, 1 - t, 6, sibling)
    finish(0)
    finish(1)
    pass_far(2)
    map_xc.wait_recv()
    map_far.wait_recv()
    logits = logits + gather(0)
    finish(2)
    logits = logits + gather(1)
    finish(3)
    logits = logits + gather(2)
    whole_side.wait_recv()
    logits = logits + (product(f_x, 3) + product(f_far, 3))

    for copy in square_copies:
        copy.wait_recv()
    square_sum = squares[0]
    for p in range(1, 8):
        square_sum = square_sum + squares[p]
    shifts = logits[ROWS : ROWS + R] * (1.0 / math.sqrt(R))
    top_part = shifts.astype(jnp.bfloat16).astype(jnp.float32)
    logits = logits[0:ROWS] + jnp.dot(
        jnp.concatenate([turned, turned], axis=1),
        jnp.concatenate([top_part, shifts - top_part], axis=0).astype(jnp.bfloat16),
        preferred_element_type=jnp.float32,
    )
    logits = logits.T * lax.rsqrt(square_sum * (1.0 / D) + 1e-05)
    top = jnp.max(logits, axis=0, keepdims=True)
    local_ids = row_ids[...] - me * logits.shape[0]
    index = lax.broadcasted_iota(jnp.int32, logits.shape, 0)
    stats[me] = jnp.zeros((1, 384), jnp.float32)
    stats[me, :, 0:ROWS] = top
    stats[me, :, 128 : 128 + ROWS] = jnp.sum(jnp.exp(logits - top), axis=0, keepdims=True)
    stats[me, :, 256 : 256 + ROWS] = jnp.sum(jnp.where(index == local_ids, logits, 0.0), axis=0, keepdims=True)
    stat_copies = exchange(stats, stat_send, stat_recv)

    loads[7].wait()
    loads[9].wait()
    for k in range(PARTS):
        blend(k)

    for copy in sent[: -len(stat_copies)]:
        copy.wait_send()

    @pl.when(inner == 0)
    def _():
        for k in range(PARTS):
            for m in range(2):
                for i in range(2):
                    share_copy(k, i, m, slot_of, 1 + m).wait_send()

    @pl.when(inner == 1)
    def _():
        for k in range(PARTS):
            for i in range(2):
                share_copy(k, i, 1 - half, slot_of, 2 - half).wait_send()
                for r in (1, 2, 3):
                    total_copy(k, i, r, half).wait_send()

    for copy in stat_copies:
        copy.wait_recv()
    every = [stats[p] for p in range(8)]
    tops = [one[:, 0:ROWS] for one in every]
    top = functools.reduce(jnp.maximum, tops)
    exp_sum = functools.reduce(
        jnp.add, [one[:, 128 : 128 + ROWS] * jnp.exp(each - top) for one, each in zip(every, tops)]
    )
    target = functools.reduce(jnp.add, [one[:, 256 : 256 + ROWS] for one in every])
    token = target - (top + jnp.log(exp_sum))
    high = token.astype(jnp.bfloat16).astype(jnp.float32)
    middle = (token - high).astype(jnp.bfloat16).astype(jnp.float32)
    thirds = jnp.concatenate([high, middle, token - high - middle, jnp.zeros((5, ROWS), jnp.float32)], axis=0)
    spread = jnp.sum(
        jnp.dot(thirds.astype(jnp.bfloat16), pick[...], preferred_element_type=jnp.float32),
        axis=0, keepdims=True,
    )
    token = jnp.concatenate([spread[:, :64], spread[:, 64:]], axis=0)
    prompt = mask[...]
    prompt_len = jnp.sum(prompt.astype(jnp.float32), axis=1, keepdims=True)
    resp = jnp.concatenate([lens[0:1, 0:1], lens[0:1, 1:2]], axis=0).astype(jnp.float32)
    position = lax.broadcasted_iota(jnp.int32, prompt.shape, 1).astype(jnp.float32)
    token = jnp.where((prompt == 0) & (position < prompt_len + resp), token, 0.0)
    token_ref[...] = token
    mean = jnp.sum(token, axis=1, keepdims=True) / resp
    mean_ref[...] = jnp.concatenate([mean[0:1], mean[1:2]], axis=1)

    for copy in stat_copies:
        copy.wait_send()


def kept_kernel(*refs):
    half = len(refs) // 2
    for source, result in zip(refs[:half], refs[half:]):
        result[...] = source[...]


def kept(arrays):
    block = pl.BlockSpec(memory_space=pltpu.VMEM)
    return pl.pallas_call(
        kept_kernel,
        out_shape=[jax.ShapeDtypeStruct(one.shape, one.dtype) for one in arrays],
        in_specs=[block] * len(arrays),
        out_specs=[block] * len(arrays),
        compiler_params=pltpu.CompilerParams(vmem_limit_bytes=8 * 1024 * 1024),
    )(*arrays)


def fused(
    grad_part, policy, ref_old, hidden_base, norm_gain, unembed, token_ids, prompt_mask, resp_len
):
    f32, bf16, i16, i32 = jnp.float32, jnp.bfloat16, jnp.int16, jnp.int32
    device_total = lax.axis_size("fsdp") * lax.axis_size("tensor") * lax.axis_size("dp")
    dma = pltpu.SemaphoreType.DMA
    outs = pl.pallas_call(
        functools.partial(fused_kernel, 8.0 / device_total),
        out_shape=[
            pltpu.VMEM((64, 1024), f32),
            pltpu.VMEM((2, 64), f32),
            pltpu.VMEM((1, 2), f32),
        ],
        in_specs=[pl.BlockSpec(memory_space=pl.ANY)] * 9,
        out_specs=[pl.BlockSpec(memory_space=pltpu.VMEM)] * 3,
        scratch_shapes=[
            pltpu.VMEM(unembed.shape, bf16),
            pltpu.VMEM((128, 2048), bf16),
            pltpu.VMEM((1, 2048), f32),
            pltpu.VMEM((64, 1024), f32),
            pltpu.VMEM((64, 1024), f32),
            pltpu.VMEM((2, 64), i32),
            pltpu.VMEM((2, 64), i32),
            pltpu.VMEM((1, 2), i32),
            pltpu.VMEM((2, 64, 4096), bf16),
            pltpu.VMEM((PARTS, 4, 64, WIDE), bf16),
            pltpu.VMEM((ROWS, 128), bf16),
            pltpu.VMEM((ROWS, 2048), bf16),
            pltpu.VMEM((1, ROWS), i32),
            pltpu.VMEM((2, PARTS, 64, WIDE), i16),
            pltpu.VMEM((2, PARTS, 1, WIDE), f32),
            pltpu.VMEM((2, PARTS, 64, WIDE), i16),
            pltpu.VMEM((2, PARTS, 1, WIDE), f32),
            pltpu.VMEM((2, PARTS, 64, WIDTH), i16),
            pltpu.VMEM((2, PARTS, 1, WIDTH), f32),
            pltpu.VMEM((2, PARTS, 64, WIDTH), i16),
            pltpu.VMEM((2, PARTS, 1, WIDTH), f32),
            pltpu.VMEM((PARTS, 64, WIDE), f32),
            pltpu.VMEM((2, PARTS, 32, WIDE), i16),
            pltpu.VMEM((2, PARTS, 1, WIDE), f32),
            pltpu.VMEM((3, PARTS, 32, WIDE), i16),
            pltpu.VMEM((3, PARTS, 1, WIDE), f32),
            pltpu.VMEM((2, PARTS, 32, WIDE), i16),
            pltpu.VMEM((2, PARTS, 1, WIDE), f32),
            pltpu.VMEM((6, 16, ROWS), f32),
            pltpu.VMEM((8, 1, ROWS), f32),
            pltpu.VMEM((4, ROWS + R, 2048), bf16),
            pltpu.VMEM((8, 1, 384), f32),
            dma((10,)), dma((PARTS, 4)), dma((PARTS, 4)), dma((2, PARTS, 2)), dma((2, PARTS, 2)), dma((2, PARTS, 2)), dma((2, PARTS, 2)),
            dma((PARTS, 2, 2)), dma((PARTS, 2, 3)), dma((PARTS, 2, 3)), dma((PARTS, 2, 2)),
            dma((8,)), dma((8,)), dma((8,)), dma((8,)),
            dma((FEEDS,)), dma((FEEDS,)), dma((7,)), dma((7,)), dma((FEEDS,)), dma((FEEDS,)), dma((FEEDS,)), dma((FEEDS,)),
            dma((1,)), dma((1,)), dma((FEEDS,)), dma((FEEDS,)), dma((8,)), dma((8,)),
        ],
        compiler_params=pltpu.CompilerParams(
            collective_id=0, has_side_effects=True, vmem_limit_bytes=56 * 1024 * 1024
        ),
    )(
        grad_part.reshape(64, 8192),
        policy.reshape(64, 1024),
        ref_old.reshape(64, 1024),
        hidden_base.reshape(128, 2048),
        norm_gain.reshape(1, 8192),
        unembed,
        token_ids.reshape(2, 64),
        prompt_mask.reshape(2, 64),
        resp_len,
    )
    outs = kept(outs)
    return (outs[0].reshape(policy.shape), outs[1].reshape(token_ids.shape), outs[2])


def solution(mesh):
    planes = (mesh.shape["fsdp"], mesh.shape["tensor"], mesh.shape["dp"])
    return jax.shard_map(
        fused if planes == (4, 2, 4) else per_device,
        mesh=mesh,
        in_specs=(
            P(("fsdp", "tensor", "dp"), None, None, None, None),
            P(None, None, None, ("fsdp", "tensor")),
            P(None, None, None, ("fsdp", "tensor")),
            P("dp", None, None, "fsdp"),
            P(),
            P(None, ("fsdp", "tensor")),
            P("dp", None, None),
            P("dp", None, None),
            P("dp", None),
        ),
        out_specs=(P(None, None, None, ("fsdp", "tensor")), P("dp", None, None), P("dp", None)),
        check_vma=False,
    )
```

```python
import functools
import math

import jax
import jax.numpy as jnp
from jax import lax
from jax.experimental import pallas as pl
from jax.experimental.pallas import tpu as pltpu
from jax.sharding import PartitionSpec as P

D = 8192
R = 16


def merged(value, axis, join):
    pieces = jax.tree.map(lambda part: lax.all_gather(part, axis), value)
    head = jax.tree.map(lambda part: part[0], pieces)
    tail = jax.tree.map(lambda part: part[1:], pieces)
    subtotal, _ = lax.scan(lambda subtotal, share: (join(subtotal, share), None), head, tail)
    return subtotal


def combine_stats(left_stats, right_stats):
    new_top = jnp.maximum(left_stats[0], right_stats[0])
    summed = left_stats[1] * jnp.exp(left_stats[0] - new_top) + right_stats[1] * jnp.exp(
        right_stats[0] - new_top
    )
    return (new_top, summed, left_stats[2] + right_stats[2])


def per_device(
    grad_part, policy, ref_old, hidden_base, norm_gain, unembed, token_ids, prompt_mask, resp_len
):
    grad_terms = grad_part[0].astype(jnp.float32)
    device_total = lax.axis_size("fsdp") * lax.axis_size("tensor") * lax.axis_size("dp")
    grad_scale = 8.0 / device_total
    grad_piece = lax.psum_scatter(grad_terms, ("fsdp", "tensor"), scatter_dimension=3, tiled=True)
    grad_total = lax.psum(grad_piece, "dp")
    ref_next = 0.4 * ref_old + 0.6 * (policy - grad_scale * grad_total)
    adapter = ref_old[ref_old.shape[0] - 1].astype(jnp.bfloat16)
    adapter_full = lax.all_gather(adapter, ("fsdp", "tensor"), axis=2, tiled=True)
    base_full = lax.all_gather(hidden_base, "fsdp", axis=3, tiled=True)
    feature_count = base_full.shape[3]
    flat_rows = base_full.reshape(-1, feature_count)
    low_rank = (
        lax.dot_general(
            flat_rows, adapter_full[0], (((1,), (1,)), ((), ())), preferred_element_type=jnp.float32
        )
        / math.sqrt(D)
    ).astype(jnp.bfloat16)
    hidden = flat_rows.astype(jnp.float32) + jnp.dot(
        low_rank, adapter_full[1], preferred_element_type=jnp.float32
    ) / math.sqrt(R)
    normed = (
        hidden * lax.rsqrt(jnp.mean(hidden * hidden, axis=1, keepdims=True) + 1e-05) * norm_gain
    ).astype(jnp.bfloat16)
    vocab_width = unembed.shape[1]
    column_start = (
        lax.axis_index("fsdp") * lax.axis_size("tensor") + lax.axis_index("tensor")
    ) * vocab_width
    column_iota = jnp.arange(vocab_width, dtype=jnp.int32)
    logits = jnp.dot(normed, unembed, preferred_element_type=jnp.float32)
    top_row = jnp.max(logits, axis=1)
    exp_row = jnp.sum(jnp.exp(logits - top_row[:, None]), axis=1)
    local_ids = token_ids.reshape(-1) - column_start
    is_target = column_iota[None, :] == local_ids[:, None]
    target_row = jnp.sum(jnp.where(is_target, logits, 0.0), axis=1)
    top_all, exp_all, target_all = merged(
        (top_row, exp_row, target_row), ("fsdp", "tensor"), combine_stats
    )
    log_total = top_all + jnp.log(exp_all)
    token_all = (target_all - log_total).reshape(token_ids.shape)
    seq_length = token_all.shape[2]
    prompt_len = jnp.sum(prompt_mask, axis=2, keepdims=True)
    position = jnp.arange(seq_length, dtype=jnp.int32)[None, None, :]
    resp_mask = (prompt_mask == 0) & (position < prompt_len + resp_len[:, :, None])
    token_logp = jnp.where(resp_mask, token_all, 0.0)
    seq_mean = jnp.sum(token_logp, axis=2) / resp_len.astype(jnp.float32)
    return (ref_next, token_logp, seq_mean)


MESH = pl.DeviceIdType.MESH
LIMIT = 32767.0


def coded(value):
    top = jnp.maximum(jnp.max(jnp.abs(value), axis=0, keepdims=True), 1e-30)
    return jnp.round(value * (LIMIT / top)).astype(jnp.int16), top * (1.0 / LIMIT)


def decoded(code, step):
    return code.astype(jnp.float32) * step


WINDOW = 48
ROWS = 2 * WINDOW


def window_rows(mask):
    start = jnp.sum(mask.astype(jnp.float32), axis=1, keepdims=True)
    row = lax.broadcasted_iota(jnp.int32, (ROWS, 128), 0)
    place = lax.broadcasted_iota(jnp.int32, (ROWS, 128), 1).astype(jnp.float32)
    source = row.astype(jnp.float32) + jnp.where(row < WINDOW, start[0:1], start[1:2] + (64.0 - WINDOW))
    return jnp.where(place == source, 1.0, 0.0)


PARTS = 2
WIDE = 1024 // PARTS
WIDTH = WIDE // 2
FEEDS = 4
SPAN = 2048 // FEEDS


def fused_kernel(
    grad_scale,
    grad_hbm, policy_hbm, ref_hbm, base_hbm, gain_hbm, unembed_hbm, ids_hbm, mask_hbm, len_hbm,
    next_ref, token_ref, mean_ref,
    unembed, base, gain, policy, ref_old, ids, mask, lens,
    grad_all, grad_in, pick, packed, row_ids, first_code, first_step, first_in_code, first_in_step,
    second_code, second_step, second_in_code, second_in_step, plane,
    part_code, part_step, share_code, share_step, total_code, total_step,
    low_rank, squares, normed, stats,
    load_sem, core_send, core_recv, first_send, first_recv, second_send, second_recv,
    share_send, share_recv, total_send, total_recv, low_send, low_recv, square_send, square_recv,
    side_send, side_recv, map_send, map_recv, x_send, x_recv, y_send, y_recv,
    own_send, own_recv, far_send, far_recv, stat_send, stat_recv,
):
    f, t, z = lax.axis_index("fsdp"), lax.axis_index("tensor"), lax.axis_index("dp")
    x, c = f // 2, f % 2
    me = f * 2 + t
    z_high, z_low = z // 2, z % 2

    def flip(bit, by):
        return bit + by - 2 * bit * by

    inner = flip(z_high, z_low)
    half = z_high
    slot_of = z_high + z_high + inner - 2 * z_high * inner

    def plane_peer(r):
        return {
            "fsdp": flip(x, r // 4) * 2 + flip(c, (r // 2) % 2),
            "tensor": flip(t, r % 2),
            "dp": z,
        }

    def stack_peer(r):
        return flip(z_high, r // 2) * 2 + flip(z_low, r % 2)

    def at_stack(index):
        return {"fsdp": f, "tensor": t, "dp": index}

    sibling, x_peer, y_peer = plane_peer(2), plane_peer(4), plane_peer(1)
    f_core, f_x, f_far = sibling["fsdp"], x_peer["fsdp"], plane_peer(6)["fsdp"]
    far_first = (5, 7, 4, 6, 1, 3, 2)

    def remote(src, dst, send, recv, peer):
        return pltpu.make_async_remote_copy(
            src_ref=src, dst_ref=dst, send_sem=send, recv_sem=recv, device_id=peer,
            device_id_type=MESH,
        )

    def lanes(start, size):
        return pl.ds(pl.multiple_of(start, 128), size)

    loads = [
        pltpu.make_async_copy(src, dst, load_sem.at[i])
        for i, (src, dst) in enumerate(
            [
                (mask_hbm, mask),
                (ids_hbm, ids),
                (base_hbm, base),
                (gain_hbm.at[:, lanes(f * 2048, 2048)], gain),
                (ref_hbm, ref_old),
                (grad_hbm.at[:, lanes(flip(x, 1) * 4096, 4096)], grad_all.at[1]),
                (grad_hbm.at[:, lanes(x * 4096, 4096)], grad_all.at[0]),
                (len_hbm, lens),
                (unembed_hbm, unembed),
                (policy_hbm, policy),
            ]
        )
    ]
    for load in loads[:8]:
        load.start()

    barrier = pltpu.get_barrier_semaphore()
    for r in range(1, 3):
        pl.semaphore_signal(
            barrier, inc=1, device_id=at_stack(stack_peer(r)), device_id_type=MESH
        )

    @pl.when(inner == 1)
    def _():
        pl.semaphore_signal(
            barrier, inc=1, device_id=at_stack(stack_peer(3)), device_id_type=MESH
        )

    for r in far_first:
        pl.semaphore_signal(barrier, inc=1, device_id=plane_peer(r), device_id_type=MESH)

    loads[0].wait()
    loads[1].wait()
    chosen = window_rows(mask[...])
    pick[...] = chosen.astype(jnp.bfloat16)
    id_row = jnp.concatenate([ids[0:1, :], ids[1:2, :]], axis=1).astype(jnp.float32)
    id_rows = lax.dot_general(
        jnp.broadcast_to(id_row, (8, 128)), chosen, (((1,), (1,)), ((), ())),
        preferred_element_type=jnp.float32, precision=lax.Precision.HIGHEST,
    )
    row_ids[...] = id_rows[0:1].astype(jnp.int32)
    loads[2].wait()
    loads[3].wait()
    for i in range(4):
        cols = slice(i * 512, (i + 1) * 512)
        rows = jnp.dot(pick[...], base[:, cols], preferred_element_type=jnp.float32)
        packed[:, cols] = rows.astype(jnp.bfloat16)
        normed[f, 0:ROWS, cols] = (rows * gain[:, cols]).astype(jnp.bfloat16)
    for load in loads[8:]:
        load.start()
    loads[4].wait()
    mine = lanes(t * 1024, 1024)
    map_rows = pl.ds(ROWS, R)
    up = ref_old[48:64, :].astype(jnp.bfloat16)
    down = ref_old[32:48, :].astype(jnp.bfloat16)
    normed[f, ROWS : ROWS + R, mine] = (up.astype(jnp.float32) * gain[:, mine]).astype(jnp.bfloat16)
    low_rank[0] = lax.dot_general(
        down, packed[:, mine], (((1,), (1,)), ((), ())), preferred_element_type=jnp.float32
    )
    loads[5].wait()
    loads[6].wait()
    pl.semaphore_wait(barrier, 9 + inner)

    sent = []

    def go(copy):
        copy.start()
        sent.append(copy)
        return copy

    pairs = [(1, 1), (1, 0), (0, 1), (0, 0)]

    def place(core, dt, k):
        return core * 2048 + flip(t, dt) * 1024 + k * WIDE

    core_copies = [{} for _ in range(PARTS)]

    def core_exchange(k):
        for dx, dt in pairs:
            slot = dx * 2 + dt
            core_copies[k][slot] = go(
                remote(
                    grad_all.at[dx, :, lanes(place(1 - c, dt, k), WIDE)], grad_in.at[k, slot],
                    core_send.at[k, slot], core_recv.at[k, slot], sibling,
                )
            )

    def rows_of(part):
        return pl.ds(pl.multiple_of(part * WINDOW, 16), WINDOW)

    def feed(src_f, part, q, send, recv, peer):
        block = normed.at[src_f, rows_of(part), q * SPAN : (q + 1) * SPAN]
        return go(remote(block, block, send, recv, peer))

    def feed_map(src_f, part, i, peer):
        block = normed.at[src_f, map_rows, lanes(part * 1024, 1024)]
        return go(remote(block, block, map_send.at[i], map_recv.at[i], peer))

    def exchange(buffer, send, recv):
        return [
            go(remote(buffer.at[me], buffer.at[me], send.at[r], recv.at[r], plane_peer(r)))
            for r in far_first
        ]

    for k in range(PARTS):
        core_exchange(k)
    from_x = []

    def low_step(i, peer):
        return go(
            remote(low_rank.at[2 * i], low_rank.at[2 * i + 1], low_send.at[i], low_recv.at[i], peer)
        )

    low_copies = [low_step(0, sibling)]
    def low_next(i, peer):
        low_copies[i - 1].wait_recv()
        low_rank[2 * i] = low_rank[2 * i - 2] + low_rank[2 * i - 1]
        low_copies.append(low_step(i, peer))

    def chip_sum(dx, dt, k, side):
        own = grad_all[dx, :, lanes(place(c, dt, k) + side * WIDTH, WIDTH)]
        other = grad_in[k, dx * 2 + dt, :, side * WIDTH : (side + 1) * WIDTH]
        return own.astype(jnp.float32) + other.astype(jnp.float32)

    def both(out_code, out_step, in_code, in_step, send, recv, side, k, peer):
        return [
            go(remote(out.at[side, k], into.at[side, k], send.at[side, k, i], recv.at[side, k, i], peer))
            for i, (out, into) in enumerate([(out_code, in_code), (out_step, in_step)])
        ]

    first_copies, second_copies = {}, {}

    def first(k):
        for slot in (3, 2, 1):
            core_copies[k][slot].wait_recv()
        for side, peer in ((0, x_peer), (1, y_peer)):
            for j in range(2):
                dx, dt = (1, j) if side == 0 else (j, 1)
                code, step = coded(chip_sum(dx, dt, k, side))
                first_code[side, k, :, j * WIDTH : (j + 1) * WIDTH] = code
                first_step[side, k, :, j * WIDTH : (j + 1) * WIDTH] = step
            first_copies[side, k] = both(
                first_code, first_step, first_in_code, first_in_step, first_send, first_recv, side, k, peer
            )

    def first_total(side, k, j):
        dx, dt = (0, j) if side == 0 else (j, 0)
        cols = slice(j * WIDTH, (j + 1) * WIDTH)
        return chip_sum(dx, dt, k, side) + decoded(
            first_in_code[side, k, :, cols], first_in_step[side, k, :, cols]
        )

    def second(k):
        core_copies[k][0].wait_recv()
        for side, peer in ((0, y_peer), (1, x_peer)):
            for copy in first_copies[side, k]:
                copy.wait_recv()
            code, step = coded(first_total(side, k, 1))
            second_code[side, k] = code
            second_step[side, k] = step
            second_copies[side, k] = both(
                second_code, second_step, second_in_code, second_in_step, second_send, second_recv,
                side, k, peer,
            )

    kinds = [(part_code, share_code), (part_step, share_step)]

    def share_copy(k, i, m, slot, target):
        out, into = kinds[i]
        return remote(
            out.at[m, k], into.at[slot, k], share_send.at[k, i, m], share_recv.at[k, i, slot], at_stack(target)
        )

    def total_copy(k, i, r, m):
        block = (total_code, total_step)[i].at[m, k]
        return remote(
            block, block, total_send.at[k, i, r - 1], total_recv.at[k, i, m], at_stack(stack_peer(r))
        )

    def share(k):
        for side in range(2):
            for copy in second_copies[side, k]:
                copy.wait_recv()
            cols = slice(side * WIDTH, (side + 1) * WIDTH)
            value = first_total(side, k, 0) + decoded(
                second_in_code[side, k], second_in_step[side, k]
            )
            plane[k, :, cols] = value
            for m in range(2):
                code, step = coded(value[m * 32 : (m + 1) * 32])
                part_code[m, k, :, cols] = code
                part_step[m, k, :, cols] = step

        @pl.when(inner == 0)
        def _():
            for m in range(2):
                for i in range(2):
                    share_copy(k, i, m, slot_of, 1 + m).start()

        @pl.when(inner == 1)
        def _():
            for i in range(2):
                share_copy(k, i, 1 - half, slot_of, 2 - half).start()

    def finish(k):
        @pl.when(inner == 1)
        def _():
            for slot in (1, 0, 2):
                for i in range(2):
                    share_copy(k, i, 1 - half, slot, 2 - half).wait_recv()
            value = plane[k, pl.ds(pl.multiple_of(half * 32, 32), 32), :]
            for slot in range(3):
                value = value + decoded(share_code[slot, k], share_step[slot, k])
            code, step = coded(value)
            total_code[half, k] = code
            total_step[half, k] = step
            for r in (1, 2, 3):
                for i in range(2):
                    total_copy(k, i, r, half).start()

    def blend(k):
        @pl.when(inner == 0)
        def _():
            for m in range(2):
                for i in range(2):
                    total_copy(k, i, 1, m).wait_recv()

        @pl.when(inner == 1)
        def _():
            for i in range(2):
                total_copy(k, i, 1, 1 - half).wait_recv()

        cols = slice(k * WIDE, (k + 1) * WIDE)
        for m in range(2):
            part = slice(m * 32, (m + 1) * 32)
            total = decoded(total_code[m, k], total_step[m, k])
            next_ref[part, cols] = 0.4 * ref_old[part, cols] + 0.6 * (
                policy[part, cols] - grad_scale * total
            )

    def product(index, q, count=1):
        rows = pl.ds(pl.multiple_of(index * 2048 + q * SPAN, SPAN), count * SPAN)
        return jnp.dot(
            normed[index, :, q * SPAN : (q + count) * SPAN], unembed[rows, :],
            preferred_element_type=jnp.float32,
        )

    from_y, from_side = [], []

    def pass_on(q):
        from_x[q].wait_recv()
        from_y.append(feed(f_x, t, q, y_send.at[q], y_recv.at[q], y_peer))
        from_side.append(feed(f_x, t, q, side_send.at[q], side_recv.at[q], sibling))

    from_far = []

    def feed_whole(src_f, send, recv, peer):
        block = normed.at[src_f, 0:ROWS, 2048 - SPAN : 2048]
        return go(remote(block, block, send, recv, peer))

    def pass_far(q):
        from_y[q].wait_recv()
        from_far.append(feed(f_x, 1 - t, q, far_send.at[q], far_recv.at[q], sibling))

    def gather(q, count=1):
        for i in range(q, q + count):
            from_side[i].wait_recv()
            from_far[i].wait_recv()
        return product(f_x, q, count) + product(f_far, q, count)
    from_x.append(feed(f, t, 0, x_send.at[0], x_recv.at[0], x_peer))
    first(0)
    first(1)
    from_x.append(feed(f, t, 1, x_send.at[1], x_recv.at[1], x_peer))
    map_y = feed_map(f, t, 0, y_peer)
    map_core = feed_map(f, t, 2, sibling)
    map_x = feed_map(f, t, 1, x_peer)
    own_rows = normed.at[f, 0:ROWS]
    from_core = go(remote(own_rows, own_rows, own_send.at[0], own_recv.at[0], sibling))
    pass_on(0)
    low_next(1, x_peer)
    second(0)
    second(1)
    from_x.append(feed(f, t, 2, x_send.at[2], x_recv.at[2], x_peer))
    from_x.append(feed_whole(f, x_send.at[3], x_recv.at[3], x_peer))
    map_y.wait_recv()
    map_side = feed_map(f, 1 - t, 3, sibling)
    loads[8].wait()
    logits = product(f, 0, FEEDS)
    map_x.wait_recv()
    map_xy = feed_map(f_x, t, 4, y_peer)
    map_xc = feed_map(f_x, t, 5, sibling)
    pass_far(0)
    pass_on(1)
    low_next(2, y_peer)
    share(0)
    for copy in (from_core, map_core, map_side):
        copy.wait_recv()
    logits = logits + product(f_core, 0, FEEDS)
    pass_on(2)
    map_xy.wait_recv()
    map_far = feed_map(f_x, 1 - t, 6, sibling)
    share(1)
    pass_far(1)
    low_copies[2].wait_recv()
    rank_sum = low_rank[4] + low_rank[5]
    turned = (rank_sum * (1.0 / math.sqrt(D))).T.astype(jnp.bfloat16)
    part_sum = jnp.zeros((ROWS, 128), jnp.float32)
    for i in range(2):
        cols = slice(i * 512, (i + 1) * 512)
        hidden = packed[:, lanes(t * 1024 + i * 512, 512)].astype(jnp.float32) + jnp.dot(
            turned, up[:, cols], preferred_element_type=jnp.float32
        ) * (1.0 / math.sqrt(R))
        square = hidden * hidden
        for j in range(4):
            part_sum = part_sum + square[:, j * 128 : (j + 1) * 128]
    squares[me] = jnp.sum(part_sum.T, axis=0, keepdims=True)
    square_copies = exchange(squares, square_send, square_recv)
    finish(0)
    from_x[3].wait_recv()
    whole_side = feed_whole(f_x, side_send.at[3], side_recv.at[3], sibling)
    map_xc.wait_recv()
    map_far.wait_recv()
    logits = logits + gather(0, 2)
    pass_far(2)
    logits = logits + product(f_x, 2, 2)
    finish(1)
    from_side[2].wait_recv()
    from_far[2].wait_recv()
    whole_side.wait_recv()
    logits = logits + product(f_far, 2, 2)

    for copy in square_copies:
        copy.wait_recv()
    square_sum = squares[0]
    for p in range(1, 8):
        square_sum = square_sum + squares[p]
    shifts = logits[ROWS : ROWS + R] * (1.0 / math.sqrt(R))
    top_part = shifts.astype(jnp.bfloat16).astype(jnp.float32)
    logits = logits[0:ROWS] + jnp.dot(
        jnp.concatenate([turned, turned], axis=1),
        jnp.concatenate([top_part, shifts - top_part], axis=0).astype(jnp.bfloat16),
        preferred_element_type=jnp.float32,
    )
    logits = logits.T * lax.rsqrt(square_sum * (1.0 / D) + 1e-05)
    top = jnp.max(logits, axis=0, keepdims=True)
    local_ids = row_ids[...] - me * logits.shape[0]
    index = lax.broadcasted_iota(jnp.int32, logits.shape, 0)
    stats[me] = jnp.zeros((1, 384), jnp.float32)
    stats[me, :, 0:ROWS] = top
    stats[me, :, 128 : 128 + ROWS] = jnp.sum(jnp.exp(logits - top), axis=0, keepdims=True)
    stats[me, :, 256 : 256 + ROWS] = jnp.sum(jnp.where(index == local_ids, logits, 0.0), axis=0, keepdims=True)
    stat_copies = exchange(stats, stat_send, stat_recv)

    loads[7].wait()
    loads[9].wait()
    for k in range(PARTS):
        blend(k)

    for copy in sent[: -len(stat_copies)]:
        copy.wait_send()

    @pl.when(inner == 0)
    def _():
        for k in range(PARTS):
            for m in range(2):
                for i in range(2):
                    share_copy(k, i, m, slot_of, 1 + m).wait_send()

    @pl.when(inner == 1)
    def _():
        for k in range(PARTS):
            for i in range(2):
                share_copy(k, i, 1 - half, slot_of, 2 - half).wait_send()
                for r in (1, 2, 3):
                    total_copy(k, i, r, half).wait_send()

    for copy in stat_copies:
        copy.wait_recv()
    every = [stats[p] for p in range(8)]
    tops = [one[:, 0:ROWS] for one in every]
    top = functools.reduce(jnp.maximum, tops)
    exp_sum = functools.reduce(
        jnp.add, [one[:, 128 : 128 + ROWS] * jnp.exp(each - top) for one, each in zip(every, tops)]
    )
    target = functools.reduce(jnp.add, [one[:, 256 : 256 + ROWS] for one in every])
    token = target - (top + jnp.log(exp_sum))
    high = token.astype(jnp.bfloat16).astype(jnp.float32)
    middle = (token - high).astype(jnp.bfloat16).astype(jnp.float32)
    thirds = jnp.concatenate([high, middle, token - high - middle, jnp.zeros((5, ROWS), jnp.float32)], axis=0)
    spread = jnp.sum(
        jnp.dot(thirds.astype(jnp.bfloat16), pick[...], preferred_element_type=jnp.float32),
        axis=0, keepdims=True,
    )
    token = jnp.concatenate([spread[:, :64], spread[:, 64:]], axis=0)
    prompt = mask[...]
    prompt_len = jnp.sum(prompt.astype(jnp.float32), axis=1, keepdims=True)
    resp = jnp.concatenate([lens[0:1, 0:1], lens[0:1, 1:2]], axis=0).astype(jnp.float32)
    position = lax.broadcasted_iota(jnp.int32, prompt.shape, 1).astype(jnp.float32)
    token = jnp.where((prompt == 0) & (position < prompt_len + resp), token, 0.0)
    token_ref[...] = token
    mean = jnp.sum(token, axis=1, keepdims=True) / resp
    mean_ref[...] = jnp.concatenate([mean[0:1], mean[1:2]], axis=1)

    for copy in stat_copies:
        copy.wait_send()


def kept_kernel(*refs):
    half = len(refs) // 2
    for source, result in zip(refs[:half], refs[half:]):
        result[...] = source[...]


def kept(arrays):
    block = pl.BlockSpec(memory_space=pltpu.VMEM)
    return pl.pallas_call(
        kept_kernel,
        out_shape=[jax.ShapeDtypeStruct(one.shape, one.dtype) for one in arrays],
        in_specs=[block] * len(arrays),
        out_specs=[block] * len(arrays),
        compiler_params=pltpu.CompilerParams(vmem_limit_bytes=8 * 1024 * 1024),
    )(*arrays)


def fused(
    grad_part, policy, ref_old, hidden_base, norm_gain, unembed, token_ids, prompt_mask, resp_len
):
    f32, bf16, i16, i32 = jnp.float32, jnp.bfloat16, jnp.int16, jnp.int32
    device_total = lax.axis_size("fsdp") * lax.axis_size("tensor") * lax.axis_size("dp")
    dma = pltpu.SemaphoreType.DMA
    outs = pl.pallas_call(
        functools.partial(fused_kernel, 8.0 / device_total),
        out_shape=[
            pltpu.VMEM((64, 1024), f32),
            pltpu.VMEM((2, 64), f32),
            pltpu.VMEM((1, 2), f32),
        ],
        in_specs=[pl.BlockSpec(memory_space=pl.ANY)] * 9,
        out_specs=[pl.BlockSpec(memory_space=pltpu.VMEM)] * 3,
        scratch_shapes=[
            pltpu.VMEM(unembed.shape, bf16),
            pltpu.VMEM((128, 2048), bf16),
            pltpu.VMEM((1, 2048), f32),
            pltpu.VMEM((64, 1024), f32),
            pltpu.VMEM((64, 1024), f32),
            pltpu.VMEM((2, 64), i32),
            pltpu.VMEM((2, 64), i32),
            pltpu.VMEM((1, 2), i32),
            pltpu.VMEM((2, 64, 4096), bf16),
            pltpu.VMEM((PARTS, 4, 64, WIDE), bf16),
            pltpu.VMEM((ROWS, 128), bf16),
            pltpu.VMEM((ROWS, 2048), bf16),
            pltpu.VMEM((1, ROWS), i32),
            pltpu.VMEM((2, PARTS, 64, WIDE), i16),
            pltpu.VMEM((2, PARTS, 1, WIDE), f32),
            pltpu.VMEM((2, PARTS, 64, WIDE), i16),
            pltpu.VMEM((2, PARTS, 1, WIDE), f32),
            pltpu.VMEM((2, PARTS, 64, WIDTH), i16),
            pltpu.VMEM((2, PARTS, 1, WIDTH), f32),
            pltpu.VMEM((2, PARTS, 64, WIDTH), i16),
            pltpu.VMEM((2, PARTS, 1, WIDTH), f32),
            pltpu.VMEM((PARTS, 64, WIDE), f32),
            pltpu.VMEM((2, PARTS, 32, WIDE), i16),
            pltpu.VMEM((2, PARTS, 1, WIDE), f32),
            pltpu.VMEM((3, PARTS, 32, WIDE), i16),
            pltpu.VMEM((3, PARTS, 1, WIDE), f32),
            pltpu.VMEM((2, PARTS, 32, WIDE), i16),
            pltpu.VMEM((2, PARTS, 1, WIDE), f32),
            pltpu.VMEM((6, 16, ROWS), f32),
            pltpu.VMEM((8, 1, ROWS), f32),
            pltpu.VMEM((4, ROWS + R, 2048), bf16),
            pltpu.VMEM((8, 1, 384), f32),
            dma((10,)), dma((PARTS, 4)), dma((PARTS, 4)), dma((2, PARTS, 2)), dma((2, PARTS, 2)), dma((2, PARTS, 2)), dma((2, PARTS, 2)),
            dma((PARTS, 2, 2)), dma((PARTS, 2, 3)), dma((PARTS, 2, 3)), dma((PARTS, 2, 2)),
            dma((8,)), dma((8,)), dma((8,)), dma((8,)),
            dma((FEEDS,)), dma((FEEDS,)), dma((7,)), dma((7,)), dma((FEEDS,)), dma((FEEDS,)), dma((FEEDS,)), dma((FEEDS,)),
            dma((1,)), dma((1,)), dma((FEEDS,)), dma((FEEDS,)), dma((8,)), dma((8,)),
        ],
        compiler_params=pltpu.CompilerParams(
            collective_id=0, has_side_effects=True, vmem_limit_bytes=56 * 1024 * 1024
        ),
    )(
        grad_part.reshape(64, 8192),
        policy.reshape(64, 1024),
        ref_old.reshape(64, 1024),
        hidden_base.reshape(128, 2048),
        norm_gain.reshape(1, 8192),
        unembed,
        token_ids.reshape(2, 64),
        prompt_mask.reshape(2, 64),
        resp_len,
    )
    outs = kept(outs)
    return (outs[0].reshape(policy.shape), outs[1].reshape(token_ids.shape), outs[2])


def solution(mesh):
    planes = (mesh.shape["fsdp"], mesh.shape["tensor"], mesh.shape["dp"])
    return jax.shard_map(
        fused if planes == (4, 2, 4) else per_device,
        mesh=mesh,
        in_specs=(
            P(("fsdp", "tensor", "dp"), None, None, None, None),
            P(None, None, None, ("fsdp", "tensor")),
            P(None, None, None, ("fsdp", "tensor")),
            P("dp", None, None, "fsdp"),
            P(),
            P(None, ("fsdp", "tensor")),
            P("dp", None, None),
            P("dp", None, None),
            P("dp", None),
        ),
        out_specs=(P(None, None, None, ("fsdp", "tensor")), P("dp", None, None), P("dp", None)),
        check_vma=False,
    )
```

```python
import functools
import math

import jax
import jax.numpy as jnp
from jax import lax
from jax.experimental import pallas as pl
from jax.experimental.pallas import tpu as pltpu
from jax.sharding import PartitionSpec as P

D = 8192
R = 16


def merged(value, axis, join):
    pieces = jax.tree.map(lambda part: lax.all_gather(part, axis), value)
    head = jax.tree.map(lambda part: part[0], pieces)
    tail = jax.tree.map(lambda part: part[1:], pieces)
    subtotal, _ = lax.scan(lambda subtotal, share: (join(subtotal, share), None), head, tail)
    return subtotal


def combine_stats(left_stats, right_stats):
    new_top = jnp.maximum(left_stats[0], right_stats[0])
    summed = left_stats[1] * jnp.exp(left_stats[0] - new_top) + right_stats[1] * jnp.exp(
        right_stats[0] - new_top
    )
    return (new_top, summed, left_stats[2] + right_stats[2])


def per_device(
    grad_part, policy, ref_old, hidden_base, norm_gain, unembed, token_ids, prompt_mask, resp_len
):
    grad_terms = grad_part[0].astype(jnp.float32)
    device_total = lax.axis_size("fsdp") * lax.axis_size("tensor") * lax.axis_size("dp")
    grad_scale = 8.0 / device_total
    grad_piece = lax.psum_scatter(grad_terms, ("fsdp", "tensor"), scatter_dimension=3, tiled=True)
    grad_total = lax.psum(grad_piece, "dp")
    ref_next = 0.4 * ref_old + 0.6 * (policy - grad_scale * grad_total)
    adapter = ref_old[ref_old.shape[0] - 1].astype(jnp.bfloat16)
    adapter_full = lax.all_gather(adapter, ("fsdp", "tensor"), axis=2, tiled=True)
    base_full = lax.all_gather(hidden_base, "fsdp", axis=3, tiled=True)
    feature_count = base_full.shape[3]
    flat_rows = base_full.reshape(-1, feature_count)
    low_rank = (
        lax.dot_general(
            flat_rows, adapter_full[0], (((1,), (1,)), ((), ())), preferred_element_type=jnp.float32
        )
        / math.sqrt(D)
    ).astype(jnp.bfloat16)
    hidden = flat_rows.astype(jnp.float32) + jnp.dot(
        low_rank, adapter_full[1], preferred_element_type=jnp.float32
    ) / math.sqrt(R)
    normed = (
        hidden * lax.rsqrt(jnp.mean(hidden * hidden, axis=1, keepdims=True) + 1e-05) * norm_gain
    ).astype(jnp.bfloat16)
    vocab_width = unembed.shape[1]
    column_start = (
        lax.axis_index("fsdp") * lax.axis_size("tensor") + lax.axis_index("tensor")
    ) * vocab_width
    column_iota = jnp.arange(vocab_width, dtype=jnp.int32)
    logits = jnp.dot(normed, unembed, preferred_element_type=jnp.float32)
    top_row = jnp.max(logits, axis=1)
    exp_row = jnp.sum(jnp.exp(logits - top_row[:, None]), axis=1)
    local_ids = token_ids.reshape(-1) - column_start
    is_target = column_iota[None, :] == local_ids[:, None]
    target_row = jnp.sum(jnp.where(is_target, logits, 0.0), axis=1)
    top_all, exp_all, target_all = merged(
        (top_row, exp_row, target_row), ("fsdp", "tensor"), combine_stats
    )
    log_total = top_all + jnp.log(exp_all)
    token_all = (target_all - log_total).reshape(token_ids.shape)
    seq_length = token_all.shape[2]
    prompt_len = jnp.sum(prompt_mask, axis=2, keepdims=True)
    position = jnp.arange(seq_length, dtype=jnp.int32)[None, None, :]
    resp_mask = (prompt_mask == 0) & (position < prompt_len + resp_len[:, :, None])
    token_logp = jnp.where(resp_mask, token_all, 0.0)
    seq_mean = jnp.sum(token_logp, axis=2) / resp_len.astype(jnp.float32)
    return (ref_next, token_logp, seq_mean)


MESH = pl.DeviceIdType.MESH
LIMIT = 32767.0


def coded(value):
    top = jnp.maximum(jnp.max(jnp.abs(value), axis=0, keepdims=True), 1e-30)
    return jnp.round(value * (LIMIT / top)).astype(jnp.int16), top * (1.0 / LIMIT)


def decoded(code, step):
    return code.astype(jnp.float32) * step


WINDOW = 48
ROWS = 2 * WINDOW


def window_rows(mask):
    start = jnp.sum(mask.astype(jnp.float32), axis=1, keepdims=True)
    row = lax.broadcasted_iota(jnp.int32, (ROWS, 128), 0)
    place = lax.broadcasted_iota(jnp.int32, (ROWS, 128), 1).astype(jnp.float32)
    source = row.astype(jnp.float32) + jnp.where(row < WINDOW, start[0:1], start[1:2] + (64.0 - WINDOW))
    return jnp.where(place == source, 1.0, 0.0)


PARTS = 2
WIDE = 1024 // PARTS
WIDTH = WIDE // 2
FEEDS = 4
SPAN = 2048 // FEEDS


def fused_kernel(
    grad_scale,
    grad_hbm, policy_hbm, ref_hbm, base_hbm, gain_hbm, unembed_hbm, ids_hbm, mask_hbm, len_hbm,
    next_ref, token_ref, mean_ref,
    unembed, base, gain, policy, ref_old, ids, mask, lens,
    grad_all, grad_in, pick, packed, row_ids, first_code, first_step, first_in_code, first_in_step,
    second_code, second_step, second_in_code, second_in_step, plane,
    part_code, part_step, share_code, share_step, total_code, total_step,
    low_rank, squares, normed, stats,
    load_sem, core_send, core_recv, first_send, first_recv, second_send, second_recv,
    share_send, share_recv, total_send, total_recv, low_send, low_recv, square_send, square_recv,
    side_send, side_recv, map_send, map_recv, x_send, x_recv, y_send, y_recv,
    own_send, own_recv, far_send, far_recv, stat_send, stat_recv,
):
    f, t, z = lax.axis_index("fsdp"), lax.axis_index("tensor"), lax.axis_index("dp")
    x, c = f // 2, f % 2
    me = f * 2 + t
    z_high, z_low = z // 2, z % 2

    def flip(bit, by):
        return bit + by - 2 * bit * by

    inner = flip(z_high, z_low)
    half = z_high
    slot_of = z_high + z_high + inner - 2 * z_high * inner

    def plane_peer(r):
        return {
            "fsdp": flip(x, r // 4) * 2 + flip(c, (r // 2) % 2),
            "tensor": flip(t, r % 2),
            "dp": z,
        }

    def stack_peer(r):
        return flip(z_high, r // 2) * 2 + flip(z_low, r % 2)

    def at_stack(index):
        return {"fsdp": f, "tensor": t, "dp": index}

    sibling, x_peer, y_peer = plane_peer(2), plane_peer(4), plane_peer(1)
    f_core, f_x, f_far = sibling["fsdp"], x_peer["fsdp"], plane_peer(6)["fsdp"]
    far_first = (5, 7, 4, 6, 1, 3, 2)

    def remote(src, dst, send, recv, peer):
        return pltpu.make_async_remote_copy(
            src_ref=src, dst_ref=dst, send_sem=send, recv_sem=recv, device_id=peer,
            device_id_type=MESH,
        )

    def lanes(start, size):
        return pl.ds(pl.multiple_of(start, 128), size)

    loads = [
        pltpu.make_async_copy(src, dst, load_sem.at[i])
        for i, (src, dst) in enumerate(
            [
                (mask_hbm, mask),
                (ids_hbm, ids),
                (base_hbm, base),
                (gain_hbm.at[:, lanes(f * 2048, 2048)], gain),
                (ref_hbm, ref_old),
                (grad_hbm.at[:, lanes(flip(x, 1) * 4096, 4096)], grad_all.at[1]),
                (grad_hbm.at[:, lanes(x * 4096, 4096)], grad_all.at[0]),
                (len_hbm, lens),
                (unembed_hbm, unembed),
                (policy_hbm, policy),
            ]
        )
    ]
    for load in loads[:8]:
        load.start()

    barrier = pltpu.get_barrier_semaphore()
    for r in range(1, 3):
        pl.semaphore_signal(
            barrier, inc=1, device_id=at_stack(stack_peer(r)), device_id_type=MESH
        )

    @pl.when(inner == 1)
    def _():
        pl.semaphore_signal(
            barrier, inc=1, device_id=at_stack(stack_peer(3)), device_id_type=MESH
        )

    for r in far_first:
        pl.semaphore_signal(barrier, inc=1, device_id=plane_peer(r), device_id_type=MESH)

    loads[0].wait()
    loads[1].wait()
    chosen = window_rows(mask[...])
    pick[...] = chosen.astype(jnp.bfloat16)
    id_row = jnp.concatenate([ids[0:1, :], ids[1:2, :]], axis=1).astype(jnp.float32)
    id_rows = lax.dot_general(
        jnp.broadcast_to(id_row, (8, 128)), chosen, (((1,), (1,)), ((), ())),
        preferred_element_type=jnp.float32, precision=lax.Precision.HIGHEST,
    )
    row_ids[...] = id_rows[0:1].astype(jnp.int32)
    loads[2].wait()
    loads[3].wait()
    for i in range(4):
        cols = slice(i * 512, (i + 1) * 512)
        rows = jnp.dot(pick[...], base[:, cols], preferred_element_type=jnp.float32)
        packed[:, cols] = rows.astype(jnp.bfloat16)
        normed[f, 0:ROWS, cols] = (rows * gain[:, cols]).astype(jnp.bfloat16)
    for load in loads[8:]:
        load.start()
    loads[4].wait()
    mine = lanes(t * 1024, 1024)
    map_rows = pl.ds(ROWS, R)
    up = ref_old[48:64, :].astype(jnp.bfloat16)
    down = ref_old[32:48, :].astype(jnp.bfloat16)
    normed[f, ROWS : ROWS + R, mine] = (up.astype(jnp.float32) * gain[:, mine]).astype(jnp.bfloat16)
    low_rank[0] = lax.dot_general(
        down, packed[:, mine], (((1,), (1,)), ((), ())), preferred_element_type=jnp.float32
    )
    loads[5].wait()
    loads[6].wait()
    pl.semaphore_wait(barrier, 9 + inner)

    sent = []

    def go(copy):
        copy.start()
        sent.append(copy)
        return copy

    pairs = [(1, 1), (1, 0), (0, 1), (0, 0)]

    def place(core, dt, k):
        return core * 2048 + flip(t, dt) * 1024 + k * WIDE

    core_copies = [{} for _ in range(PARTS)]

    def core_exchange(k):
        for dx, dt in pairs:
            slot = dx * 2 + dt
            core_copies[k][slot] = go(
                remote(
                    grad_all.at[dx, :, lanes(place(1 - c, dt, k), WIDE)], grad_in.at[k, slot],
                    core_send.at[k, slot], core_recv.at[k, slot], sibling,
                )
            )

    def rows_of(part):
        return pl.ds(pl.multiple_of(part * WINDOW, 16), WINDOW)

    def feed(src_f, part, q, send, recv, peer):
        block = normed.at[src_f, rows_of(part), q * SPAN : (q + 1) * SPAN]
        return go(remote(block, block, send, recv, peer))

    def feed_map(src_f, part, i, peer):
        block = normed.at[src_f, map_rows, lanes(part * 1024, 1024)]
        return go(remote(block, block, map_send.at[i], map_recv.at[i], peer))

    def exchange(buffer, send, recv):
        return [
            go(remote(buffer.at[me], buffer.at[me], send.at[r], recv.at[r], plane_peer(r)))
            for r in far_first
        ]

    for k in range(PARTS):
        core_exchange(k)
    from_x = []

    def low_step(i, peer):
        return go(
            remote(low_rank.at[2 * i], low_rank.at[2 * i + 1], low_send.at[i], low_recv.at[i], peer)
        )

    low_copies = [low_step(0, sibling)]
    def low_next(i, peer):
        low_copies[i - 1].wait_recv()
        low_rank[2 * i] = low_rank[2 * i - 2] + low_rank[2 * i - 1]
        low_copies.append(low_step(i, peer))

    def chip_sum(dx, dt, k, side):
        own = grad_all[dx, :, lanes(place(c, dt, k) + side * WIDTH, WIDTH)]
        other = grad_in[k, dx * 2 + dt, :, side * WIDTH : (side + 1) * WIDTH]
        return own.astype(jnp.float32) + other.astype(jnp.float32)

    def both(out_code, out_step, in_code, in_step, send, recv, side, k, peer):
        return [
            go(remote(out.at[side, k], into.at[side, k], send.at[side, k, i], recv.at[side, k, i], peer))
            for i, (out, into) in enumerate([(out_code, in_code), (out_step, in_step)])
        ]

    first_copies, second_copies = {}, {}

    def first(k):
        for slot in (3, 2, 1):
            core_copies[k][slot].wait_recv()
        for side, peer in ((0, x_peer), (1, y_peer)):
            for j in range(2):
                dx, dt = (1, j) if side == 0 else (j, 1)
                code, step = coded(chip_sum(dx, dt, k, side))
                first_code[side, k, :, j * WIDTH : (j + 1) * WIDTH] = code
                first_step[side, k, :, j * WIDTH : (j + 1) * WIDTH] = step
            first_copies[side, k] = both(
                first_code, first_step, first_in_code, first_in_step, first_send, first_recv, side, k, peer
            )

    def first_total(side, k, j):
        dx, dt = (0, j) if side == 0 else (j, 0)
        cols = slice(j * WIDTH, (j + 1) * WIDTH)
        return chip_sum(dx, dt, k, side) + decoded(
            first_in_code[side, k, :, cols], first_in_step[side, k, :, cols]
        )

    def second(k):
        core_copies[k][0].wait_recv()
        for side, peer in ((0, y_peer), (1, x_peer)):
            for copy in first_copies[side, k]:
                copy.wait_recv()
            code, step = coded(first_total(side, k, 1))
            second_code[side, k] = code
            second_step[side, k] = step
            second_copies[side, k] = both(
                second_code, second_step, second_in_code, second_in_step, second_send, second_recv,
                side, k, peer,
            )

    kinds = [(part_code, share_code), (part_step, share_step)]

    def share_copy(k, i, m, slot, target):
        out, into = kinds[i]
        return remote(
            out.at[m, k], into.at[slot, k], share_send.at[k, i, m], share_recv.at[k, i, slot], at_stack(target)
        )

    def total_copy(k, i, r, m):
        block = (total_code, total_step)[i].at[m, k]
        return remote(
            block, block, total_send.at[k, i, r - 1], total_recv.at[k, i, m], at_stack(stack_peer(r))
        )

    def share(k):
        for side in range(2):
            for copy in second_copies[side, k]:
                copy.wait_recv()
            cols = slice(side * WIDTH, (side + 1) * WIDTH)
            value = first_total(side, k, 0) + decoded(
                second_in_code[side, k], second_in_step[side, k]
            )
            plane[k, :, cols] = value
            for m in range(2):
                code, step = coded(value[m * 32 : (m + 1) * 32])
                part_code[m, k, :, cols] = code
                part_step[m, k, :, cols] = step

        @pl.when(inner == 0)
        def _():
            for m in range(2):
                for i in range(2):
                    share_copy(k, i, m, slot_of, 1 + m).start()

        @pl.when(inner == 1)
        def _():
            for i in range(2):
                share_copy(k, i, 1 - half, slot_of, 2 - half).start()

    def finish(k):
        @pl.when(inner == 1)
        def _():
            for slot in (1, 0, 2):
                for i in range(2):
                    share_copy(k, i, 1 - half, slot, 2 - half).wait_recv()
            value = plane[k, pl.ds(pl.multiple_of(half * 32, 32), 32), :]
            for slot in range(3):
                value = value + decoded(share_code[slot, k], share_step[slot, k])
            code, step = coded(value)
            total_code[half, k] = code
            total_step[half, k] = step
            for r in (1, 2, 3):
                for i in range(2):
                    total_copy(k, i, r, half).start()

    def blend(k):
        @pl.when(inner == 0)
        def _():
            for m in range(2):
                for i in range(2):
                    total_copy(k, i, 1, m).wait_recv()

        @pl.when(inner == 1)
        def _():
            for i in range(2):
                total_copy(k, i, 1, 1 - half).wait_recv()

        cols = slice(k * WIDE, (k + 1) * WIDE)
        for m in range(2):
            part = slice(m * 32, (m + 1) * 32)
            total = decoded(total_code[m, k], total_step[m, k])
            next_ref[part, cols] = 0.4 * ref_old[part, cols] + 0.6 * (
                policy[part, cols] - grad_scale * total
            )

    def product(index, q, count=1):
        rows = pl.ds(pl.multiple_of(index * 2048 + q * SPAN, SPAN), count * SPAN)
        return jnp.dot(
            normed[index, :, q * SPAN : (q + count) * SPAN], unembed[rows, :],
            preferred_element_type=jnp.float32,
        )

    from_y, from_side = [], []

    def pass_on(q):
        from_x[q].wait_recv()
        from_y.append(feed(f_x, t, q, y_send.at[q], y_recv.at[q], y_peer))
        from_side.append(feed(f_x, t, q, side_send.at[q], side_recv.at[q], sibling))

    from_far = []

    def feed_whole(src_f, send, recv, peer):
        block = normed.at[src_f, 0:ROWS, 2048 - SPAN : 2048]
        return go(remote(block, block, send, recv, peer))

    def pass_far(q):
        from_y[q].wait_recv()
        from_far.append(feed(f_x, 1 - t, q, far_send.at[q], far_recv.at[q], sibling))

    def gather(q, count=1):
        for i in range(q, q + count):
            from_side[i].wait_recv()
            from_far[i].wait_recv()
        return product(f_x, q, count) + product(f_far, q, count)
    from_x.append(feed(f, t, 0, x_send.at[0], x_recv.at[0], x_peer))
    first(0)
    first(1)
    from_x.append(feed(f, t, 1, x_send.at[1], x_recv.at[1], x_peer))
    map_y = feed_map(f, t, 0, y_peer)
    map_core = feed_map(f, t, 2, sibling)
    map_x = feed_map(f, t, 1, x_peer)
    own_rows = normed.at[f, 0:ROWS]
    from_core = go(remote(own_rows, own_rows, own_send.at[0], own_recv.at[0], sibling))
    pass_on(0)
    low_next(1, x_peer)
    second(0)
    second(1)
    from_x.append(feed(f, t, 2, x_send.at[2], x_recv.at[2], x_peer))
    from_x.append(feed_whole(f, x_send.at[3], x_recv.at[3], x_peer))
    map_y.wait_recv()
    map_side = feed_map(f, 1 - t, 3, sibling)
    loads[8].wait()
    logits = product(f, 0, FEEDS)
    map_x.wait_recv()
    map_xy = feed_map(f_x, t, 4, y_peer)
    map_xc = feed_map(f_x, t, 5, sibling)
    pass_far(0)
    pass_on(1)
    low_next(2, y_peer)
    share(0)
    for copy in (from_core, map_core, map_side):
        copy.wait_recv()
    logits = logits + product(f_core, 0, FEEDS)
    pass_on(2)
    map_xy.wait_recv()
    map_far = feed_map(f_x, 1 - t, 6, sibling)
    share(1)
    pass_far(1)
    low_copies[2].wait_recv()
    rank_sum = low_rank[4] + low_rank[5]
    turned = (rank_sum * (1.0 / math.sqrt(D))).T.astype(jnp.bfloat16)
    part_sum = jnp.zeros((ROWS, 128), jnp.float32)
    for i in range(2):
        cols = slice(i * 512, (i + 1) * 512)
        hidden = packed[:, lanes(t * 1024 + i * 512, 512)].astype(jnp.float32) + jnp.dot(
            turned, up[:, cols], preferred_element_type=jnp.float32
        ) * (1.0 / math.sqrt(R))
        square = hidden * hidden
        for j in range(4):
            part_sum = part_sum + square[:, j * 128 : (j + 1) * 128]
    squares[me] = jnp.sum(part_sum.T, axis=0, keepdims=True)
    square_copies = exchange(squares, square_send, square_recv)
    finish(0)
    from_x[3].wait_recv()
    whole_side = feed_whole(f_x, side_send.at[3], side_recv.at[3], sibling)
    map_xc.wait_recv()
    map_far.wait_recv()
    logits = logits + gather(0, 2)
    pass_far(2)
    logits = logits + product(f_x, 2, 2)
    finish(1)
    from_side[2].wait_recv()
    from_far[2].wait_recv()
    whole_side.wait_recv()
    logits = logits + product(f_far, 2, 2)

    for copy in square_copies:
        copy.wait_recv()
    square_sum = squares[0]
    for p in range(1, 8):
        square_sum = square_sum + squares[p]
    shifts = logits[ROWS : ROWS + R] * (1.0 / math.sqrt(R))
    top_part = shifts.astype(jnp.bfloat16).astype(jnp.float32)
    logits = logits[0:ROWS] + jnp.dot(
        jnp.concatenate([turned, turned], axis=1),
        jnp.concatenate([top_part, shifts - top_part], axis=0).astype(jnp.bfloat16),
        preferred_element_type=jnp.float32,
    )
    logits = logits.T * lax.rsqrt(square_sum * (1.0 / D) + 1e-05)
    top = jnp.max(logits, axis=0, keepdims=True)
    local_ids = row_ids[...] - me * logits.shape[0]
    index = lax.broadcasted_iota(jnp.int32, logits.shape, 0)
    stats[me] = jnp.zeros((1, 384), jnp.float32)
    stats[me, :, 0:ROWS] = top
    stats[me, :, 128 : 128 + ROWS] = jnp.sum(jnp.exp(logits - top), axis=0, keepdims=True)
    stats[me, :, 256 : 256 + ROWS] = jnp.sum(jnp.where(index == local_ids, logits, 0.0), axis=0, keepdims=True)
    stat_copies = exchange(stats, stat_send, stat_recv)

    loads[7].wait()
    loads[9].wait()
    for k in range(PARTS):
        blend(k)

    for copy in sent[: -len(stat_copies)]:
        copy.wait_send()

    @pl.when(inner == 0)
    def _():
        for k in range(PARTS):
            for m in range(2):
                for i in range(2):
                    share_copy(k, i, m, slot_of, 1 + m).wait_send()

    @pl.when(inner == 1)
    def _():
        for k in range(PARTS):
            for i in range(2):
                share_copy(k, i, 1 - half, slot_of, 2 - half).wait_send()
                for r in (1, 2, 3):
                    total_copy(k, i, r, half).wait_send()

    for copy in stat_copies:
        copy.wait_recv()
    every = [stats[p] for p in range(8)]
    tops = [one[:, 0:ROWS] for one in every]
    top = functools.reduce(jnp.maximum, tops)
    exp_sum = functools.reduce(
        jnp.add, [one[:, 128 : 128 + ROWS] * jnp.exp(each - top) for one, each in zip(every, tops)]
    )
    target = functools.reduce(jnp.add, [one[:, 256 : 256 + ROWS] for one in every])
    token = target - (top + jnp.log(exp_sum))
    high = token.astype(jnp.bfloat16).astype(jnp.float32)
    middle = (token - high).astype(jnp.bfloat16).astype(jnp.float32)
    thirds = jnp.concatenate([high, middle, token - high - middle, jnp.zeros((5, ROWS), jnp.float32)], axis=0)
    spread = jnp.sum(
        jnp.dot(thirds.astype(jnp.bfloat16), pick[...], preferred_element_type=jnp.float32),
        axis=0, keepdims=True,
    )
    token = jnp.concatenate([spread[:, :64], spread[:, 64:]], axis=0)
    prompt = mask[...]
    prompt_len = jnp.sum(prompt.astype(jnp.float32), axis=1, keepdims=True)
    resp = jnp.concatenate([lens[0:1, 0:1], lens[0:1, 1:2]], axis=0).astype(jnp.float32)
    position = lax.broadcasted_iota(jnp.int32, prompt.shape, 1).astype(jnp.float32)
    token = jnp.where((prompt == 0) & (position < prompt_len + resp), token, 0.0)
    token_ref[...] = token
    mean = jnp.sum(token, axis=1, keepdims=True) / resp
    mean_ref[...] = jnp.concatenate([mean[0:1], mean[1:2]], axis=1)

    for copy in stat_copies:
        copy.wait_send()


def kept_kernel(*refs):
    count = (len(refs) - 1) // 2
    copies = [
        pltpu.make_async_copy(refs[i], refs[count + i], refs[-1].at[i]) for i in range(count)
    ]
    for copy in copies:
        copy.start()
    for copy in copies:
        copy.wait()


def kept(arrays):
    return pl.pallas_call(
        kept_kernel,
        out_shape=[jax.ShapeDtypeStruct(one.shape, one.dtype) for one in arrays],
        in_specs=[pl.BlockSpec(memory_space=pltpu.VMEM)] * len(arrays),
        out_specs=[pl.BlockSpec(memory_space=pl.ANY)] * len(arrays),
        scratch_shapes=[pltpu.SemaphoreType.DMA((len(arrays),))],
        compiler_params=pltpu.CompilerParams(vmem_limit_bytes=8 * 1024 * 1024),
    )(*arrays)


def fused(
    grad_part, policy, ref_old, hidden_base, norm_gain, unembed, token_ids, prompt_mask, resp_len
):
    f32, bf16, i16, i32 = jnp.float32, jnp.bfloat16, jnp.int16, jnp.int32
    device_total = lax.axis_size("fsdp") * lax.axis_size("tensor") * lax.axis_size("dp")
    dma = pltpu.SemaphoreType.DMA
    outs = pl.pallas_call(
        functools.partial(fused_kernel, 8.0 / device_total),
        out_shape=[
            pltpu.VMEM((64, 1024), f32),
            pltpu.VMEM((2, 64), f32),
            pltpu.VMEM((1, 2), f32),
        ],
        in_specs=[pl.BlockSpec(memory_space=pl.ANY)] * 9,
        out_specs=[pl.BlockSpec(memory_space=pltpu.VMEM)] * 3,
        scratch_shapes=[
            pltpu.VMEM(unembed.shape, bf16),
            pltpu.VMEM((128, 2048), bf16),
            pltpu.VMEM((1, 2048), f32),
            pltpu.VMEM((64, 1024), f32),
            pltpu.VMEM((64, 1024), f32),
            pltpu.VMEM((2, 64), i32),
            pltpu.VMEM((2, 64), i32),
            pltpu.VMEM((1, 2), i32),
            pltpu.VMEM((2, 64, 4096), bf16),
            pltpu.VMEM((PARTS, 4, 64, WIDE), bf16),
            pltpu.VMEM((ROWS, 128), bf16),
            pltpu.VMEM((ROWS, 2048), bf16),
            pltpu.VMEM((1, ROWS), i32),
            pltpu.VMEM((2, PARTS, 64, WIDE), i16),
            pltpu.VMEM((2, PARTS, 1, WIDE), f32),
            pltpu.VMEM((2, PARTS, 64, WIDE), i16),
            pltpu.VMEM((2, PARTS, 1, WIDE), f32),
            pltpu.VMEM((2, PARTS, 64, WIDTH), i16),
            pltpu.VMEM((2, PARTS, 1, WIDTH), f32),
            pltpu.VMEM((2, PARTS, 64, WIDTH), i16),
            pltpu.VMEM((2, PARTS, 1, WIDTH), f32),
            pltpu.VMEM((PARTS, 64, WIDE), f32),
            pltpu.VMEM((2, PARTS, 32, WIDE), i16),
            pltpu.VMEM((2, PARTS, 1, WIDE), f32),
            pltpu.VMEM((3, PARTS, 32, WIDE), i16),
            pltpu.VMEM((3, PARTS, 1, WIDE), f32),
            pltpu.VMEM((2, PARTS, 32, WIDE), i16),
            pltpu.VMEM((2, PARTS, 1, WIDE), f32),
            pltpu.VMEM((6, 16, ROWS), f32),
            pltpu.VMEM((8, 1, ROWS), f32),
            pltpu.VMEM((4, ROWS + R, 2048), bf16),
            pltpu.VMEM((8, 1, 384), f32),
            dma((10,)), dma((PARTS, 4)), dma((PARTS, 4)), dma((2, PARTS, 2)), dma((2, PARTS, 2)), dma((2, PARTS, 2)), dma((2, PARTS, 2)),
            dma((PARTS, 2, 2)), dma((PARTS, 2, 3)), dma((PARTS, 2, 3)), dma((PARTS, 2, 2)),
            dma((8,)), dma((8,)), dma((8,)), dma((8,)),
            dma((FEEDS,)), dma((FEEDS,)), dma((7,)), dma((7,)), dma((FEEDS,)), dma((FEEDS,)), dma((FEEDS,)), dma((FEEDS,)),
            dma((1,)), dma((1,)), dma((FEEDS,)), dma((FEEDS,)), dma((8,)), dma((8,)),
        ],
        compiler_params=pltpu.CompilerParams(
            collective_id=0, has_side_effects=True, vmem_limit_bytes=56 * 1024 * 1024
        ),
    )(
        grad_part.reshape(64, 8192),
        policy.reshape(64, 1024),
        ref_old.reshape(64, 1024),
        hidden_base.reshape(128, 2048),
        norm_gain.reshape(1, 8192),
        unembed,
        token_ids.reshape(2, 64),
        prompt_mask.reshape(2, 64),
        resp_len,
    )
    outs = kept(outs)
    return (outs[0].reshape(policy.shape), outs[1].reshape(token_ids.shape), outs[2])


def solution(mesh):
    planes = (mesh.shape["fsdp"], mesh.shape["tensor"], mesh.shape["dp"])
    return jax.shard_map(
        fused if planes == (4, 2, 4) else per_device,
        mesh=mesh,
        in_specs=(
            P(("fsdp", "tensor", "dp"), None, None, None, None),
            P(None, None, None, ("fsdp", "tensor")),
            P(None, None, None, ("fsdp", "tensor")),
            P("dp", None, None, "fsdp"),
            P(),
            P(None, ("fsdp", "tensor")),
            P("dp", None, None),
            P("dp", None, None),
            P("dp", None),
        ),
        out_specs=(P(None, None, None, ("fsdp", "tensor")), P("dp", None, None), P("dp", None)),
        check_vma=False,
    )
```

```python
import functools
import math

import jax
import jax.numpy as jnp
from jax import lax
from jax.experimental import pallas as pl
from jax.experimental.pallas import tpu as pltpu
from jax.sharding import PartitionSpec as P

D = 8192
R = 16


def merged(value, axis, join):
    pieces = jax.tree.map(lambda part: lax.all_gather(part, axis), value)
    head = jax.tree.map(lambda part: part[0], pieces)
    tail = jax.tree.map(lambda part: part[1:], pieces)
    subtotal, _ = lax.scan(lambda subtotal, share: (join(subtotal, share), None), head, tail)
    return subtotal


def combine_stats(left_stats, right_stats):
    new_top = jnp.maximum(left_stats[0], right_stats[0])
    summed = left_stats[1] * jnp.exp(left_stats[0] - new_top) + right_stats[1] * jnp.exp(
        right_stats[0] - new_top
    )
    return (new_top, summed, left_stats[2] + right_stats[2])


def per_device(
    grad_part, policy, ref_old, hidden_base, norm_gain, unembed, token_ids, prompt_mask, resp_len
):
    grad_terms = grad_part[0].astype(jnp.float32)
    device_total = lax.axis_size("fsdp") * lax.axis_size("tensor") * lax.axis_size("dp")
    grad_scale = 8.0 / device_total
    grad_piece = lax.psum_scatter(grad_terms, ("fsdp", "tensor"), scatter_dimension=3, tiled=True)
    grad_total = lax.psum(grad_piece, "dp")
    ref_next = 0.4 * ref_old + 0.6 * (policy - grad_scale * grad_total)
    adapter = ref_old[ref_old.shape[0] - 1].astype(jnp.bfloat16)
    adapter_full = lax.all_gather(adapter, ("fsdp", "tensor"), axis=2, tiled=True)
    base_full = lax.all_gather(hidden_base, "fsdp", axis=3, tiled=True)
    feature_count = base_full.shape[3]
    flat_rows = base_full.reshape(-1, feature_count)
    low_rank = (
        lax.dot_general(
            flat_rows, adapter_full[0], (((1,), (1,)), ((), ())), preferred_element_type=jnp.float32
        )
        / math.sqrt(D)
    ).astype(jnp.bfloat16)
    hidden = flat_rows.astype(jnp.float32) + jnp.dot(
        low_rank, adapter_full[1], preferred_element_type=jnp.float32
    ) / math.sqrt(R)
    normed = (
        hidden * lax.rsqrt(jnp.mean(hidden * hidden, axis=1, keepdims=True) + 1e-05) * norm_gain
    ).astype(jnp.bfloat16)
    vocab_width = unembed.shape[1]
    column_start = (
        lax.axis_index("fsdp") * lax.axis_size("tensor") + lax.axis_index("tensor")
    ) * vocab_width
    column_iota = jnp.arange(vocab_width, dtype=jnp.int32)
    logits = jnp.dot(normed, unembed, preferred_element_type=jnp.float32)
    top_row = jnp.max(logits, axis=1)
    exp_row = jnp.sum(jnp.exp(logits - top_row[:, None]), axis=1)
    local_ids = token_ids.reshape(-1) - column_start
    is_target = column_iota[None, :] == local_ids[:, None]
    target_row = jnp.sum(jnp.where(is_target, logits, 0.0), axis=1)
    top_all, exp_all, target_all = merged(
        (top_row, exp_row, target_row), ("fsdp", "tensor"), combine_stats
    )
    log_total = top_all + jnp.log(exp_all)
    token_all = (target_all - log_total).reshape(token_ids.shape)
    seq_length = token_all.shape[2]
    prompt_len = jnp.sum(prompt_mask, axis=2, keepdims=True)
    position = jnp.arange(seq_length, dtype=jnp.int32)[None, None, :]
    resp_mask = (prompt_mask == 0) & (position < prompt_len + resp_len[:, :, None])
    token_logp = jnp.where(resp_mask, token_all, 0.0)
    seq_mean = jnp.sum(token_logp, axis=2) / resp_len.astype(jnp.float32)
    return (ref_next, token_logp, seq_mean)


MESH = pl.DeviceIdType.MESH
LIMIT = 32767.0


def coded(value):
    top = jnp.maximum(jnp.max(jnp.abs(value), axis=0, keepdims=True), 1e-30)
    return jnp.round(value * (LIMIT / top)).astype(jnp.int16), top * (1.0 / LIMIT)


def decoded(code, step):
    return code.astype(jnp.float32) * step


WINDOW = 48
ROWS = 2 * WINDOW


def window_rows(mask):
    start = jnp.sum(mask.astype(jnp.float32), axis=1, keepdims=True)
    row = lax.broadcasted_iota(jnp.int32, (ROWS, 128), 0)
    place = lax.broadcasted_iota(jnp.int32, (ROWS, 128), 1).astype(jnp.float32)
    source = row.astype(jnp.float32) + jnp.where(row < WINDOW, start[0:1], start[1:2] + (64.0 - WINDOW))
    return jnp.where(place == source, 1.0, 0.0)


PARTS = 2
WIDE = 1024 // PARTS
WIDTH = WIDE // 2
FEEDS = 4
SPAN = 2048 // FEEDS


def fused_kernel(
    grad_scale,
    grad_hbm, policy_hbm, ref_hbm, base_hbm, gain_hbm, unembed_hbm, ids_hbm, mask_hbm, len_hbm,
    next_ref, token_ref, mean_ref,
    unembed, base, gain, policy, ref_old, ids, mask, lens,
    grad_all, grad_in, pick, packed, row_ids, first_code, first_step, first_in_code, first_in_step,
    second_code, second_step, second_in_code, second_in_step, plane,
    part_code, part_step, share_code, share_step, total_code, total_step,
    low_rank, squares, normed, stats,
    load_sem, core_send, core_recv, first_send, first_recv, second_send, second_recv,
    share_send, share_recv, total_send, total_recv, low_send, low_recv, square_send, square_recv,
    side_send, side_recv, map_send, map_recv, x_send, x_recv, y_send, y_recv,
    own_send, own_recv, far_send, far_recv, stat_send, stat_recv,
):
    f, t, z = lax.axis_index("fsdp"), lax.axis_index("tensor"), lax.axis_index("dp")
    x, c = f // 2, f % 2
    me = f * 2 + t
    z_high, z_low = z // 2, z % 2

    def flip(bit, by):
        return bit + by - 2 * bit * by

    inner = flip(z_high, z_low)
    half = z_high
    slot_of = z_high + z_high + inner - 2 * z_high * inner

    def plane_peer(r):
        return {
            "fsdp": flip(x, r // 4) * 2 + flip(c, (r // 2) % 2),
            "tensor": flip(t, r % 2),
            "dp": z,
        }

    def stack_peer(r):
        return flip(z_high, r // 2) * 2 + flip(z_low, r % 2)

    def at_stack(index):
        return {"fsdp": f, "tensor": t, "dp": index}

    sibling, x_peer, y_peer = plane_peer(2), plane_peer(4), plane_peer(1)
    f_core, f_x, f_far = sibling["fsdp"], x_peer["fsdp"], plane_peer(6)["fsdp"]
    far_first = (5, 7, 4, 6, 1, 3, 2)

    def remote(src, dst, send, recv, peer):
        return pltpu.make_async_remote_copy(
            src_ref=src, dst_ref=dst, send_sem=send, recv_sem=recv, device_id=peer,
            device_id_type=MESH,
        )

    def lanes(start, size):
        return pl.ds(pl.multiple_of(start, 128), size)

    loads = [
        pltpu.make_async_copy(src, dst, load_sem.at[i])
        for i, (src, dst) in enumerate(
            [
                (mask_hbm, mask),
                (ids_hbm, ids),
                (base_hbm, base),
                (gain_hbm.at[:, lanes(f * 2048, 2048)], gain),
                (ref_hbm, ref_old),
                (grad_hbm.at[:, lanes(flip(x, 1) * 4096, 4096)], grad_all.at[1]),
                (grad_hbm.at[:, lanes(x * 4096, 4096)], grad_all.at[0]),
                (len_hbm, lens),
                (unembed_hbm, unembed),
                (policy_hbm, policy),
            ]
        )
    ]
    for load in loads[:8]:
        load.start()

    barrier = pltpu.get_barrier_semaphore()
    for r in range(1, 3):
        pl.semaphore_signal(
            barrier, inc=1, device_id=at_stack(stack_peer(r)), device_id_type=MESH
        )

    @pl.when(inner == 1)
    def _():
        pl.semaphore_signal(
            barrier, inc=1, device_id=at_stack(stack_peer(3)), device_id_type=MESH
        )

    for r in far_first:
        pl.semaphore_signal(barrier, inc=1, device_id=plane_peer(r), device_id_type=MESH)

    loads[0].wait()
    loads[1].wait()
    chosen = window_rows(mask[...])
    pick[...] = chosen.astype(jnp.bfloat16)
    id_row = jnp.concatenate([ids[0:1, :], ids[1:2, :]], axis=1).astype(jnp.float32)
    id_rows = lax.dot_general(
        jnp.broadcast_to(id_row, (8, 128)), chosen, (((1,), (1,)), ((), ())),
        preferred_element_type=jnp.float32, precision=lax.Precision.HIGHEST,
    )
    row_ids[...] = id_rows[0:1].astype(jnp.int32)
    loads[2].wait()
    loads[3].wait()
    for i in range(4):
        cols = slice(i * 512, (i + 1) * 512)
        rows = jnp.dot(pick[...], base[:, cols], preferred_element_type=jnp.float32)
        packed[:, cols] = rows.astype(jnp.bfloat16)
        normed[f, 0:ROWS, cols] = (rows * gain[:, cols]).astype(jnp.bfloat16)
    for load in loads[8:]:
        load.start()
    loads[4].wait()
    mine = lanes(t * 1024, 1024)
    map_rows = pl.ds(ROWS, R)
    up = ref_old[48:64, :].astype(jnp.bfloat16)
    down = ref_old[32:48, :].astype(jnp.bfloat16)
    normed[f, ROWS : ROWS + R, mine] = (up.astype(jnp.float32) * gain[:, mine]).astype(jnp.bfloat16)
    low_rank[0] = lax.dot_general(
        down, packed[:, mine], (((1,), (1,)), ((), ())), preferred_element_type=jnp.float32
    )
    loads[5].wait()
    loads[6].wait()
    pl.semaphore_wait(barrier, 9 + inner)

    sent = []

    def go(copy):
        copy.start()
        sent.append(copy)
        return copy

    pairs = [(1, 1), (1, 0), (0, 1), (0, 0)]

    def place(core, dt, k):
        return core * 2048 + flip(t, dt) * 1024 + k * WIDE

    core_copies = [{} for _ in range(PARTS)]

    def core_exchange(k):
        for dx, dt in pairs:
            slot = dx * 2 + dt
            core_copies[k][slot] = go(
                remote(
                    grad_all.at[dx, :, lanes(place(1 - c, dt, k), WIDE)], grad_in.at[k, slot],
                    core_send.at[k, slot], core_recv.at[k, slot], sibling,
                )
            )

    def rows_of(part):
        return pl.ds(pl.multiple_of(part * WINDOW, 16), WINDOW)

    def feed(src_f, part, q, send, recv, peer):
        block = normed.at[src_f, rows_of(part), q * SPAN : (q + 1) * SPAN]
        return go(remote(block, block, send, recv, peer))

    def feed_map(src_f, part, i, peer):
        block = normed.at[src_f, map_rows, lanes(part * 1024, 1024)]
        return go(remote(block, block, map_send.at[i], map_recv.at[i], peer))

    def exchange(buffer, send, recv):
        return [
            go(remote(buffer.at[me], buffer.at[me], send.at[r], recv.at[r], plane_peer(r)))
            for r in far_first
        ]

    for k in range(PARTS):
        core_exchange(k)
    from_x = []

    def low_step(i, peer):
        return go(
            remote(low_rank.at[2 * i], low_rank.at[2 * i + 1], low_send.at[i], low_recv.at[i], peer)
        )

    low_copies = [low_step(0, sibling)]
    def low_next(i, peer):
        low_copies[i - 1].wait_recv()
        low_rank[2 * i] = low_rank[2 * i - 2] + low_rank[2 * i - 1]
        low_copies.append(low_step(i, peer))

    def chip_sum(dx, dt, k, side):
        own = grad_all[dx, :, lanes(place(c, dt, k) + side * WIDTH, WIDTH)]
        other = grad_in[k, dx * 2 + dt, :, side * WIDTH : (side + 1) * WIDTH]
        return own.astype(jnp.float32) + other.astype(jnp.float32)

    def both(out_code, out_step, in_code, in_step, send, recv, side, k, peer):
        return [
            go(remote(out.at[side, k], into.at[side, k], send.at[side, k, i], recv.at[side, k, i], peer))
            for i, (out, into) in enumerate([(out_code, in_code), (out_step, in_step)])
        ]

    first_copies, second_copies = {}, {}

    def first(k):
        for slot in (3, 2, 1):
            core_copies[k][slot].wait_recv()
        for side, peer in ((0, x_peer), (1, y_peer)):
            for j in range(2):
                dx, dt = (1, j) if side == 0 else (j, 1)
                code, step = coded(chip_sum(dx, dt, k, side))
                first_code[side, k, :, j * WIDTH : (j + 1) * WIDTH] = code
                first_step[side, k, :, j * WIDTH : (j + 1) * WIDTH] = step
            first_copies[side, k] = both(
                first_code, first_step, first_in_code, first_in_step, first_send, first_recv, side, k, peer
            )

    def first_total(side, k, j):
        dx, dt = (0, j) if side == 0 else (j, 0)
        cols = slice(j * WIDTH, (j + 1) * WIDTH)
        return chip_sum(dx, dt, k, side) + decoded(
            first_in_code[side, k, :, cols], first_in_step[side, k, :, cols]
        )

    def second(k):
        core_copies[k][0].wait_recv()
        for side, peer in ((0, y_peer), (1, x_peer)):
            for copy in first_copies[side, k]:
                copy.wait_recv()
            code, step = coded(first_total(side, k, 1))
            second_code[side, k] = code
            second_step[side, k] = step
            second_copies[side, k] = both(
                second_code, second_step, second_in_code, second_in_step, second_send, second_recv,
                side, k, peer,
            )

    kinds = [(part_code, share_code), (part_step, share_step)]

    def share_copy(k, i, m, slot, target):
        out, into = kinds[i]
        return remote(
            out.at[m, k], into.at[slot, k], share_send.at[k, i, m], share_recv.at[k, i, slot], at_stack(target)
        )

    def total_copy(k, i, r, m):
        block = (total_code, total_step)[i].at[m, k]
        return remote(
            block, block, total_send.at[k, i, r - 1], total_recv.at[k, i, m], at_stack(stack_peer(r))
        )

    def share(k):
        for side in range(2):
            for copy in second_copies[side, k]:
                copy.wait_recv()
            cols = slice(side * WIDTH, (side + 1) * WIDTH)
            value = first_total(side, k, 0) + decoded(
                second_in_code[side, k], second_in_step[side, k]
            )
            plane[k, :, cols] = value
            for m in range(2):
                code, step = coded(value[m * 32 : (m + 1) * 32])
                part_code[m, k, :, cols] = code
                part_step[m, k, :, cols] = step

        @pl.when(inner == 0)
        def _():
            for m in range(2):
                for i in range(2):
                    share_copy(k, i, m, slot_of, 1 + m).start()

        @pl.when(inner == 1)
        def _():
            for i in range(2):
                share_copy(k, i, 1 - half, slot_of, 2 - half).start()

    def finish(k):
        @pl.when(inner == 1)
        def _():
            for slot in (1, 0, 2):
                for i in range(2):
                    share_copy(k, i, 1 - half, slot, 2 - half).wait_recv()
            value = plane[k, pl.ds(pl.multiple_of(half * 32, 32), 32), :]
            for slot in range(3):
                value = value + decoded(share_code[slot, k], share_step[slot, k])
            code, step = coded(value)
            total_code[half, k] = code
            total_step[half, k] = step
            for r in (1, 2, 3):
                for i in range(2):
                    total_copy(k, i, r, half).start()

    def blend(k):
        @pl.when(inner == 0)
        def _():
            for m in range(2):
                for i in range(2):
                    total_copy(k, i, 1, m).wait_recv()

        @pl.when(inner == 1)
        def _():
            for i in range(2):
                total_copy(k, i, 1, 1 - half).wait_recv()

        cols = slice(k * WIDE, (k + 1) * WIDE)
        for m in range(2):
            part = slice(m * 32, (m + 1) * 32)
            total = decoded(total_code[m, k], total_step[m, k])
            next_ref[part, cols] = 0.4 * ref_old[part, cols] + 0.6 * (
                policy[part, cols] - grad_scale * total
            )

    def product(index, q, count=1):
        rows = pl.ds(pl.multiple_of(index * 2048 + q * SPAN, SPAN), count * SPAN)
        return jnp.dot(
            normed[index, :, q * SPAN : (q + count) * SPAN], unembed[rows, :],
            preferred_element_type=jnp.float32,
        )

    from_y, from_side = [], []

    def pass_on(q):
        from_x[q].wait_recv()
        from_y.append(feed(f_x, t, q, y_send.at[q], y_recv.at[q], y_peer))
        from_side.append(feed(f_x, t, q, side_send.at[q], side_recv.at[q], sibling))

    from_far = []

    def feed_whole(src_f, send, recv, peer):
        block = normed.at[src_f, 0:ROWS, 2048 - SPAN : 2048]
        return go(remote(block, block, send, recv, peer))

    def pass_far(q):
        from_y[q].wait_recv()
        from_far.append(feed(f_x, 1 - t, q, far_send.at[q], far_recv.at[q], sibling))

    def gather(q, count=1):
        for i in range(q, q + count):
            from_side[i].wait_recv()
            from_far[i].wait_recv()
        return product(f_x, q, count) + product(f_far, q, count)
    from_x.append(feed(f, t, 0, x_send.at[0], x_recv.at[0], x_peer))
    first(0)
    first(1)
    map_y = feed_map(f, t, 0, y_peer)
    map_core = feed_map(f, t, 2, sibling)
    from_x.append(feed(f, t, 1, x_send.at[1], x_recv.at[1], x_peer))
    map_x = feed_map(f, t, 1, x_peer)
    own_rows = normed.at[f, 0:ROWS]
    from_core = go(remote(own_rows, own_rows, own_send.at[0], own_recv.at[0], sibling))
    pass_on(0)
    low_next(1, x_peer)
    from_x.append(feed(f, t, 2, x_send.at[2], x_recv.at[2], x_peer))
    second(0)
    second(1)
    from_x.append(feed_whole(f, x_send.at[3], x_recv.at[3], x_peer))
    map_y.wait_recv()
    map_side = feed_map(f, 1 - t, 3, sibling)
    loads[8].wait()
    logits = product(f, 0, FEEDS)
    map_x.wait_recv()
    map_xy = feed_map(f_x, t, 4, y_peer)
    map_xc = feed_map(f_x, t, 5, sibling)
    pass_far(0)
    pass_on(1)
    low_next(2, y_peer)
    share(0)
    pass_on(2)
    for copy in (from_core, map_core, map_side):
        copy.wait_recv()
    logits = logits + product(f_core, 0, FEEDS)
    share(1)
    map_xy.wait_recv()
    map_far = feed_map(f_x, 1 - t, 6, sibling)
    pass_far(1)
    low_copies[2].wait_recv()
    rank_sum = low_rank[4] + low_rank[5]
    turned = (rank_sum * (1.0 / math.sqrt(D))).T.astype(jnp.bfloat16)
    part_sum = jnp.zeros((ROWS, 128), jnp.float32)
    for i in range(2):
        cols = slice(i * 512, (i + 1) * 512)
        hidden = packed[:, lanes(t * 1024 + i * 512, 512)].astype(jnp.float32) + jnp.dot(
            turned, up[:, cols], preferred_element_type=jnp.float32
        ) * (1.0 / math.sqrt(R))
        square = hidden * hidden
        for j in range(4):
            part_sum = part_sum + square[:, j * 128 : (j + 1) * 128]
    squares[me] = jnp.sum(part_sum.T, axis=0, keepdims=True)
    square_copies = exchange(squares, square_send, square_recv)
    from_x[3].wait_recv()
    whole_side = feed_whole(f_x, side_send.at[3], side_recv.at[3], sibling)
    finish(0)
    pass_far(2)
    map_xc.wait_recv()
    map_far.wait_recv()
    logits = logits + gather(0, 2)
    logits = logits + product(f_x, 2, 2)
    finish(1)
    from_side[2].wait_recv()
    from_far[2].wait_recv()
    whole_side.wait_recv()
    logits = logits + product(f_far, 2, 2)

    for copy in square_copies:
        copy.wait_recv()
    square_sum = squares[0]
    for p in range(1, 8):
        square_sum = square_sum + squares[p]
    shifts = logits[ROWS : ROWS + R] * (1.0 / math.sqrt(R))
    top_part = shifts.astype(jnp.bfloat16).astype(jnp.float32)
    logits = logits[0:ROWS] + jnp.dot(
        jnp.concatenate([turned, turned], axis=1),
        jnp.concatenate([top_part, shifts - top_part], axis=0).astype(jnp.bfloat16),
        preferred_element_type=jnp.float32,
    )
    logits = logits.T * lax.rsqrt(square_sum * (1.0 / D) + 1e-05)
    top = jnp.max(logits, axis=0, keepdims=True)
    local_ids = row_ids[...] - me * logits.shape[0]
    index = lax.broadcasted_iota(jnp.int32, logits.shape, 0)
    stats[me] = jnp.zeros((1, 384), jnp.float32)
    stats[me, :, 0:ROWS] = top
    stats[me, :, 128 : 128 + ROWS] = jnp.sum(jnp.exp(logits - top), axis=0, keepdims=True)
    stats[me, :, 256 : 256 + ROWS] = jnp.sum(jnp.where(index == local_ids, logits, 0.0), axis=0, keepdims=True)
    stat_copies = exchange(stats, stat_send, stat_recv)

    loads[7].wait()
    loads[9].wait()
    for k in range(PARTS):
        blend(k)

    for copy in sent[: -len(stat_copies)]:
        copy.wait_send()

    @pl.when(inner == 0)
    def _():
        for k in range(PARTS):
            for m in range(2):
                for i in range(2):
                    share_copy(k, i, m, slot_of, 1 + m).wait_send()

    @pl.when(inner == 1)
    def _():
        for k in range(PARTS):
            for i in range(2):
                share_copy(k, i, 1 - half, slot_of, 2 - half).wait_send()
                for r in (1, 2, 3):
                    total_copy(k, i, r, half).wait_send()

    for copy in stat_copies:
        copy.wait_recv()
    every = [stats[p] for p in range(8)]
    tops = [one[:, 0:ROWS] for one in every]
    top = functools.reduce(jnp.maximum, tops)
    exp_sum = functools.reduce(
        jnp.add, [one[:, 128 : 128 + ROWS] * jnp.exp(each - top) for one, each in zip(every, tops)]
    )
    target = functools.reduce(jnp.add, [one[:, 256 : 256 + ROWS] for one in every])
    token = target - (top + jnp.log(exp_sum))
    high = token.astype(jnp.bfloat16).astype(jnp.float32)
    middle = (token - high).astype(jnp.bfloat16).astype(jnp.float32)
    thirds = jnp.concatenate([high, middle, token - high - middle, jnp.zeros((5, ROWS), jnp.float32)], axis=0)
    spread = jnp.sum(
        jnp.dot(thirds.astype(jnp.bfloat16), pick[...], preferred_element_type=jnp.float32),
        axis=0, keepdims=True,
    )
    token = jnp.concatenate([spread[:, :64], spread[:, 64:]], axis=0)
    prompt = mask[...]
    prompt_len = jnp.sum(prompt.astype(jnp.float32), axis=1, keepdims=True)
    resp = jnp.concatenate([lens[0:1, 0:1], lens[0:1, 1:2]], axis=0).astype(jnp.float32)
    position = lax.broadcasted_iota(jnp.int32, prompt.shape, 1).astype(jnp.float32)
    token = jnp.where((prompt == 0) & (position < prompt_len + resp), token, 0.0)
    token_ref[...] = token
    mean = jnp.sum(token, axis=1, keepdims=True) / resp
    mean_ref[...] = jnp.concatenate([mean[0:1], mean[1:2]], axis=1)

    for copy in stat_copies:
        copy.wait_send()


def kept_kernel(*refs):
    half = len(refs) // 2
    for source, result in zip(refs[:half], refs[half:]):
        result[...] = source[...]


def kept(arrays):
    block = pl.BlockSpec(memory_space=pltpu.VMEM)
    return pl.pallas_call(
        kept_kernel,
        out_shape=[jax.ShapeDtypeStruct(one.shape, one.dtype) for one in arrays],
        in_specs=[block] * len(arrays),
        out_specs=[block] * len(arrays),
        compiler_params=pltpu.CompilerParams(vmem_limit_bytes=8 * 1024 * 1024),
    )(*arrays)


def fused(
    grad_part, policy, ref_old, hidden_base, norm_gain, unembed, token_ids, prompt_mask, resp_len
):
    f32, bf16, i16, i32 = jnp.float32, jnp.bfloat16, jnp.int16, jnp.int32
    device_total = lax.axis_size("fsdp") * lax.axis_size("tensor") * lax.axis_size("dp")
    dma = pltpu.SemaphoreType.DMA
    outs = pl.pallas_call(
        functools.partial(fused_kernel, 8.0 / device_total),
        out_shape=[
            pltpu.VMEM((64, 1024), f32),
            pltpu.VMEM((2, 64), f32),
            pltpu.VMEM((1, 2), f32),
        ],
        in_specs=[pl.BlockSpec(memory_space=pl.ANY)] * 9,
        out_specs=[pl.BlockSpec(memory_space=pltpu.VMEM)] * 3,
        scratch_shapes=[
            pltpu.VMEM(unembed.shape, bf16),
            pltpu.VMEM((128, 2048), bf16),
            pltpu.VMEM((1, 2048), f32),
            pltpu.VMEM((64, 1024), f32),
            pltpu.VMEM((64, 1024), f32),
            pltpu.VMEM((2, 64), i32),
            pltpu.VMEM((2, 64), i32),
            pltpu.VMEM((1, 2), i32),
            pltpu.VMEM((2, 64, 4096), bf16),
            pltpu.VMEM((PARTS, 4, 64, WIDE), bf16),
            pltpu.VMEM((ROWS, 128), bf16),
            pltpu.VMEM((ROWS, 2048), bf16),
            pltpu.VMEM((1, ROWS), i32),
            pltpu.VMEM((2, PARTS, 64, WIDE), i16),
            pltpu.VMEM((2, PARTS, 1, WIDE), f32),
            pltpu.VMEM((2, PARTS, 64, WIDE), i16),
            pltpu.VMEM((2, PARTS, 1, WIDE), f32),
            pltpu.VMEM((2, PARTS, 64, WIDTH), i16),
            pltpu.VMEM((2, PARTS, 1, WIDTH), f32),
            pltpu.VMEM((2, PARTS, 64, WIDTH), i16),
            pltpu.VMEM((2, PARTS, 1, WIDTH), f32),
            pltpu.VMEM((PARTS, 64, WIDE), f32),
            pltpu.VMEM((2, PARTS, 32, WIDE), i16),
            pltpu.VMEM((2, PARTS, 1, WIDE), f32),
            pltpu.VMEM((3, PARTS, 32, WIDE), i16),
            pltpu.VMEM((3, PARTS, 1, WIDE), f32),
            pltpu.VMEM((2, PARTS, 32, WIDE), i16),
            pltpu.VMEM((2, PARTS, 1, WIDE), f32),
            pltpu.VMEM((6, 16, ROWS), f32),
            pltpu.VMEM((8, 1, ROWS), f32),
            pltpu.VMEM((4, ROWS + R, 2048), bf16),
            pltpu.VMEM((8, 1, 384), f32),
            dma((10,)), dma((PARTS, 4)), dma((PARTS, 4)), dma((2, PARTS, 2)), dma((2, PARTS, 2)), dma((2, PARTS, 2)), dma((2, PARTS, 2)),
            dma((PARTS, 2, 2)), dma((PARTS, 2, 3)), dma((PARTS, 2, 3)), dma((PARTS, 2, 2)),
            dma((8,)), dma((8,)), dma((8,)), dma((8,)),
            dma((FEEDS,)), dma((FEEDS,)), dma((7,)), dma((7,)), dma((FEEDS,)), dma((FEEDS,)), dma((FEEDS,)), dma((FEEDS,)),
            dma((1,)), dma((1,)), dma((FEEDS,)), dma((FEEDS,)), dma((8,)), dma((8,)),
        ],
        compiler_params=pltpu.CompilerParams(
            collective_id=0, has_side_effects=True, vmem_limit_bytes=56 * 1024 * 1024
        ),
    )(
        grad_part.reshape(64, 8192),
        policy.reshape(64, 1024),
        ref_old.reshape(64, 1024),
        hidden_base.reshape(128, 2048),
        norm_gain.reshape(1, 8192),
        unembed,
        token_ids.reshape(2, 64),
        prompt_mask.reshape(2, 64),
        resp_len,
    )
    outs = kept(outs)
    return (outs[0].reshape(policy.shape), outs[1].reshape(token_ids.shape), outs[2])


def solution(mesh):
    planes = (mesh.shape["fsdp"], mesh.shape["tensor"], mesh.shape["dp"])
    return jax.shard_map(
        fused if planes == (4, 2, 4) else per_device,
        mesh=mesh,
        in_specs=(
            P(("fsdp", "tensor", "dp"), None, None, None, None),
            P(None, None, None, ("fsdp", "tensor")),
            P(None, None, None, ("fsdp", "tensor")),
            P("dp", None, None, "fsdp"),
            P(),
            P(None, ("fsdp", "tensor")),
            P("dp", None, None),
            P("dp", None, None),
            P("dp", None),
        ),
        out_specs=(P(None, None, None, ("fsdp", "tensor")), P("dp", None, None), P("dp", None)),
        check_vma=False,
    )
```
